512 devices in a mesh: blk: 64 (over y_hi, z, x), src: 8 (over y_lo, core).
Axes of the slice: x: 4, y: 8 (y_hi: 2, y_lo: 4; y = y_hi * 4 + y_lo), z: 8, core: 2. Of those that a mesh axis runs over, the one named last changes fastest.
Arguments:
- raw_records: float32 [8192, 10240], P('blk', 'src'), may hold values from -6 to 6
- fir_taps: float32 [64], replicated, may hold values from -0.75 to 0.75
- alive_mask: int32 [8192], P('blk'), may hold values 0 or 1
- source_index: int32 [64, 2], P('blk'), may hold values from 0 to 127
Outputs:
- correlations: bfloat16 [128, 8192, 512], P('src', 'blk')
The draws below stay inside these ranges and needn't reach their ends.
All inputs are finite; a program needn't handle non-finite values. No bound on the sum of `alive_mask` on one device may be relied on, other than what follows from the above.
Results may differ from the reference program's by a relative error of at most 0.0053.
Values sent between devices are 32-bit elements; how exact they have to be, the bound alone decides.
A program may use at most 128 MiB of HBM per device.

```python
import math
import jax
import jax.numpy as jnp
from jax import lax

VS = 2
S = 512
NFFT = 1024
LAGS = 512
TAPS = 64
DEC = 20
HALF = 64
RAW = 10240
CB = 128
BLOCKS = 64
CHANNELS = 8192
NSRC = 128


def touch_ends(drawn, rng, smallest, high):
    extent = drawn.shape
    index_at = [jax.random.randint(jax.random.fold_in(rng, axis), (), 0, extent[axis]) for axis in range(len(extent))]
    drawn = drawn.at[tuple(index_at)].set(smallest)
    longest = extent.index(max(extent))
    index_at[longest] = (index_at[longest] + 1) % extent[longest]
    return drawn.at[tuple(index_at)].set(high)


def shard_levels(key, shape, pieces, smallest, high):
    factor_of = 1.0
    for axis_at, blocks in pieces:
        steps = jax.random.uniform(jax.random.fold_in(jax.random.fold_in(key, 6), axis_at), (blocks,), jnp.float32, smallest / len(pieces), high / len(pieces))
        factor_of = factor_of * jnp.repeat(jnp.exp(steps), shape[axis_at] // blocks).reshape((-1,) + (1,) * (len(shape) - 1 - axis_at))
    return factor_of


def noise(rng, extent, width, most, cuts=(), kind=jnp.bfloat16):
    values = width * jax.random.normal(rng, extent, jnp.float32)
    if cuts:
        values = values * shard_levels(rng, extent, cuts, -0.22, 0.18)
    return jnp.clip(values, -most, most).astype(kind)


def setup_inputs(seed: int = 0) -> dict:
    arg_keys = jax.random.split(jax.random.key(seed), 5)
    return {
        "raw_records": noise(arg_keys[0], (CHANNELS, RAW), 1.0, 6.0, ((0, 64), (1, 8)), jnp.float32),
        "fir_taps": noise(arg_keys[1], (TAPS,), TAPS ** -0.5, 0.75, (), jnp.float32),
        "alive_mask": touch_ends((jax.random.randint(arg_keys[2], (CHANNELS,), 0, 8) < 7).astype(jnp.int32), jax.random.fold_in(arg_keys[2], 1), 0, 1),
        "source_index": touch_ends(jax.random.randint(arg_keys[3], (BLOCKS, VS), 0, CB), jax.random.fold_in(arg_keys[3], 1), 0, CB - 1).astype(jnp.int32),
    }


def decimate(records, fir_taps, out_count):
    tap_groups = -(-TAPS // DEC)
    needed = DEC * (out_count + tap_groups - 1)
    padded = jnp.pad(records, ((0, 0), (0, DEC * tap_groups)))[:, :needed]
    sample_blocks = padded.reshape(padded.shape[0], out_count + tap_groups - 1, DEC)
    tap_rows = jnp.pad(fir_taps, (0, tap_groups * DEC - TAPS)).reshape(tap_groups, DEC)
    filtered = jnp.zeros((padded.shape[0], out_count), jnp.float32)
    for tap_group in range(tap_groups):
        filtered = filtered + jnp.einsum('cnm,m->cn', sample_blocks[:, tap_group:tap_group + out_count], tap_rows[tap_group], precision=lax.Precision.HIGHEST)
    return filtered

def forward_table():
    sample_times = jnp.arange(S, dtype=jnp.int32)[:, None]
    bin_index = jnp.arange(NFFT // 2, dtype=jnp.int32)[None, :]
    phases = 2.0 * math.pi / NFFT * (sample_times * bin_index % NFFT).astype(jnp.float32)
    return jnp.concatenate([jnp.cos(phases), -jnp.sin(phases)], axis=1)

def band_table():
    half_bins = NFFT // 2
    row_bins = jnp.arange(half_bins, dtype=jnp.int32)[:, None]
    col_bins = jnp.arange(half_bins, dtype=jnp.int32)[None, :]
    band_mask = (jnp.abs(row_bins - col_bins) <= HALF).astype(jnp.float32)
    return (band_mask, lax.optimization_barrier(jnp.sum(band_mask, axis=0)))

def whiten(series, alive_rows):
    spectrum = jnp.dot(series, forward_table(), precision=lax.Precision.HIGHEST)
    half_bins = spectrum.shape[1] // 2
    real_part = spectrum[:, :half_bins]
    imag_part = spectrum[:, half_bins:]
    power_bins = real_part * real_part + imag_part * imag_part
    band_mask, band_count = band_table()
    smooth = jnp.dot(power_bins, band_mask, precision=lax.Precision.HIGHEST) / band_count
    inverse_amp = alive_rows[:, None] / jnp.sqrt(smooth + 1e-06)
    return spectrum * jnp.concatenate([inverse_amp, inverse_amp], axis=1)

def lag_table():
    half_bins = NFFT // 2
    bin_index = jnp.arange(half_bins, dtype=jnp.int32)[:, None]
    lag_shift = jnp.arange(LAGS, dtype=jnp.int32)[None, :] - LAGS // 2
    phases = 2.0 * math.pi / NFFT * (bin_index * lag_shift % NFFT).astype(jnp.float32)
    bin_weight = jnp.where(bin_index == 0, 0.5, 1.0).astype(jnp.float32) / math.sqrt(half_bins)
    return jnp.concatenate([bin_weight * jnp.cos(phases), -bin_weight * jnp.sin(phases)], axis=0).astype(jnp.bfloat16)

def reference(raw_records, fir_taps, alive_mask, source_index):
    series = decimate(raw_records, fir_taps, S)
    spectra = whiten(series, alive_mask.astype(jnp.float32))
    offsets = (jnp.arange(BLOCKS, dtype=jnp.int32) * CB)[:, None]
    source_channel = source_index.astype(jnp.int32) + offsets
    lag_weights = lag_table().astype(jnp.float32)
    half_bins = NFFT // 2
    receivers = jnp.arange(CHANNELS, dtype=jnp.int32)

    def group_corr(group_channels):
        sources = spectra[group_channels]
        src_re = sources[:, None, :half_bins]
        src_im = sources[:, None, half_bins:]
        rec_re = spectra[None, :, :half_bins]
        rec_im = spectra[None, :, half_bins:]
        cross_spec = jnp.concatenate([src_re * rec_re + src_im * rec_im, src_re * rec_im - src_im * rec_re], axis=2).astype(jnp.bfloat16)
        flat_cross = cross_spec.reshape(VS * CHANNELS, 2 * half_bins).astype(jnp.float32)
        lagged = jnp.dot(flat_cross, lag_weights, preferred_element_type=jnp.float32).reshape(VS, CHANNELS, LAGS)
        self_pair = receivers[None, :] == group_channels[:, None]
        return jnp.where(self_pair[:, :, None], 0.0, lagged).astype(jnp.bfloat16)
    stacked = lax.map(group_corr, source_channel)
    return stacked.reshape(NSRC, CHANNELS, LAGS)
```

```python
import functools
import math

import jax
import jax.numpy as jnp
import ml_dtypes
import numpy as np
from jax import lax
from jax.experimental import pallas as pl
from jax.experimental.pallas import tpu as pltpu
from jax.sharding import PartitionSpec as P

S = 512
NFFT = 1024
BINS = NFFT // 2
LAGS = 512
TAPS = 64
DEC = 20
HALF = 64
LANES = 128
EDGE = 8
MESH = pl.DeviceIdType.MESH
F32 = jnp.float32
BF16 = jnp.bfloat16


def split_np(table):
    high = table.astype(np.float32).astype(ml_dtypes.bfloat16)
    low = (table - high.astype(np.float64)).astype(ml_dtypes.bfloat16)
    return high, low


def forward_tables():
    phases = 2.0 * math.pi / NFFT * (np.outer(np.arange(S), np.arange(BINS)) % NFFT)
    return split_np(np.concatenate([np.cos(phases), -np.sin(phases)], axis=1))


def band_table():
    bins = np.arange(BINS)
    return (np.abs(bins[:, None] - bins[None, :]) <= HALF).astype(ml_dtypes.bfloat16)


def lag_table():
    bins = np.arange(BINS)
    shift = np.arange(LAGS) - LAGS // 2
    phases = 2.0 * math.pi / NFFT * (np.outer(bins, shift) % NFFT)
    weight = np.where(bins[:, None] == 0, 0.5, 1.0) / math.sqrt(BINS)
    table = np.concatenate([weight * np.cos(phases), -weight * np.sin(phases)], axis=0)
    return table.astype(np.float32).astype(ml_dtypes.bfloat16)


def split(value):
    high = value.astype(BF16)
    return high, (value - high.astype(F32)).astype(BF16)


def dot(a, b):
    return jnp.dot(a, b, preferred_element_type=F32)


def dot_nt(a, b):
    return lax.dot_general(a, b, (((1,), (1,)), ((), ())), preferred_element_type=F32)


def whitened(series, high_table, low_table, band):
    rows = series.shape[0]
    high, low = split(series)
    both = dot(jnp.concatenate([high, low], axis=0), high_table)
    spectrum = both[:rows] + both[rows:] + dot(high, low_table)
    real_part, imag_part = spectrum[:, :BINS], spectrum[:, BINS:]
    high, low = split(real_part * real_part + imag_part * imag_part)
    sums = dot(jnp.concatenate([high, low], axis=0), band)
    bins = lax.broadcasted_iota(jnp.int32, (1, BINS), 1)
    count = jnp.minimum(bins, HALF) + jnp.minimum(BINS - 1 - bins, HALF) + 1
    smooth = (sums[:rows] + sums[rows:]) / count.astype(F32)
    factor = lax.rsqrt(smooth + 1e-6)
    return real_part * factor, imag_part * factor


def tap_matrix(taps, raw_count, rows, edge_row):
    row = lax.broadcasted_iota(jnp.int32, (rows, LANES), 0)
    start = DEC * jnp.where(row < edge_row, row, row - rows)
    lane = lax.broadcasted_iota(jnp.int32, (rows, LANES), 1)
    spread = jnp.broadcast_to(taps, (rows, LANES))
    turned = jnp.take_along_axis(spread, (lane - start) & (LANES - 1), axis=1)
    high, low = split(turned)
    high, low = high.astype(F32), low.astype(F32)
    highs, lows = [], []
    for first in range(0, raw_count, LANES):
        offset = lane + first - start
        inside = (offset >= 0) & (offset < TAPS)
        highs.append(jnp.where(inside, high, 0.0).astype(BF16))
        lows.append(jnp.where(inside, low, 0.0).astype(BF16))
    return jnp.concatenate(highs, axis=1), jnp.concatenate(lows, axis=1)


def gather_kernel(
    shards,
    raw_hbm,
    taps_ref,
    alive_ref,
    index_ref,
    high_hbm,
    low_hbm,
    band_hbm,
    receivers_ref,
    sources_ref,
    raw,
    high_table,
    low_table,
    band,
    parts,
    pieces,
    packed,
    arrived,
    local_sem,
    piece_send,
    piece_recv,
    part_send,
    part_recv,
    source_send,
    source_recv,
):
    blk = lax.axis_index("blk")
    src = lax.axis_index("src")
    channels, raw_count = raw.shape
    out_rows = S // shards
    group = lax.div(blk, shards)
    slot = lax.rem(blk, shards)

    barrier = pltpu.get_barrier_semaphore()
    for step in range(1, shards):
        peer = lax.rem(src + step, shards)
        pl.semaphore_signal(barrier, inc=1, device_id=(blk, peer), device_id_type=MESH)
    for step in range(shards):
        @pl.when((group != src) | (slot != step))
        def _():
            pl.semaphore_signal(
                barrier, inc=1, device_id=(src * shards + step, group), device_id_type=MESH
            )

    loads = [
        pltpu.make_async_copy(source, target, local_sem.at[k])
        for k, (source, target) in enumerate(
            [(raw_hbm, raw), (high_hbm, high_table), (low_hbm, low_table), (band_hbm, band)]
        )
    ]
    for load in loads:
        load.start()

    tap_high, tap_low = tap_matrix(taps_ref[...], raw_count, out_rows + EDGE, out_rows)
    loads[0].wait()
    raw_high, raw_low = split(raw[...])
    decimated = dot_nt(tap_high, raw_high) + dot_nt(tap_low, raw_high) + dot_nt(tap_high, raw_low)
    decimated = decimated * alive_ref[...].astype(F32)
    parts[src] = decimated

    lane = lax.broadcasted_iota(jnp.int32, (8, channels), 1)
    row = lax.broadcasted_iota(jnp.int32, (8, channels), 0)
    chosen = jnp.where(row == 0, index_ref[0, 0], jnp.where(row == 1, index_ref[0, 1], -1))
    chooser = (lane == chosen).astype(F32).astype(BF16)
    padded = jnp.concatenate(
        [
            decimated[:out_rows],
            jnp.zeros((LANES - out_rows - EDGE, channels), F32),
            decimated[out_rows:],
        ],
        axis=0,
    )
    first, rest = split(padded)
    second, third = split(padded - first.astype(F32))
    pieces[src] = dot_nt(chooser, first) + dot_nt(chooser, second) + dot_nt(chooser, third)

    @pl.when(group != src)
    def _():
        pl.semaphore_wait(barrier, 2 * shards - 1)

    @pl.when(group == src)
    def _():
        pl.semaphore_wait(barrier, 2 * shards - 2)

    def piece_copy(step):
        return pltpu.make_async_remote_copy(
            src_ref=pieces.at[src],
            dst_ref=pieces.at[src],
            send_sem=piece_send.at[step],
            recv_sem=piece_recv.at[step],
            device_id=(blk, lax.rem(src + step, shards)),
            device_id_type=MESH,
        )

    def part_copy(step):
        return pltpu.make_async_remote_copy(
            src_ref=parts.at[src],
            dst_ref=parts.at[src],
            send_sem=part_send.at[step],
            recv_sem=part_recv.at[step],
            device_id=(blk, lax.rem(src + step, shards)),
            device_id_type=MESH,
        )

    def source_copy(step):
        return pltpu.make_async_remote_copy(
            src_ref=packed,
            dst_ref=arrived.at[slot],
            send_sem=source_send.at[step],
            recv_sem=source_recv.at[slot],
            device_id=(src * shards + step, group),
            device_id_type=MESH,
        )

    def source_arrival(step):
        return pltpu.make_async_remote_copy(
            src_ref=packed,
            dst_ref=arrived.at[step],
            send_sem=source_send.at[step],
            recv_sem=source_recv.at[step],
            device_id=(src * shards + step, group),
            device_id_type=MESH,
        )

    for step in range(1, shards):
        piece_copy(step).start()
    for step in range(1, shards):
        part_copy(step).start()

    for step in range(1, shards):
        piece_copy(step).wait_recv()
    lane = lax.broadcasted_iota(jnp.int32, (8, LANES), 1)
    for pair in range(shards // 2):
        after = pieces[2 * pair + 2] if 2 * pair + 2 < shards else jnp.zeros((8, LANES), F32)
        joined = pltpu.roll(pieces[2 * pair + 1], LANES // 2, 1) + jnp.where(
            lane < LANES // 2, pieces[2 * pair], after
        )
        packed[pair : pair + 1, :] = joined[0:1]
        packed[shards // 2 + pair : shards // 2 + pair + 1, :] = joined[1:2]

    for step in range(shards):
        me = (group == src) & (slot == step)

        @pl.when(me)
        def _():
            arrived[step] = packed[...]

        @pl.when(jnp.logical_not(me))
        def _():
            source_copy(step).start()

    for load in loads[1:]:
        load.wait()
    for step in range(shards):
        @pl.when((group != src) | (slot != step))
        def _():
            source_arrival(step).wait_recv()

    half = shards // 2
    sources = jnp.concatenate(
        [
            jnp.concatenate([arrived[:, v * half + pair, :] for pair in range(half)], axis=1)
            for v in range(2)
        ],
        axis=0,
    )
    real_part, imag_part = whitened(sources, high_table[...], low_table[...], band[...])
    sources_ref[:, :BINS] = real_part
    sources_ref[:, BINS:] = imag_part

    for step in range(1, shards):
        part_copy(step).wait_recv()
    rows = []
    for shard in range(shards):
        rows.append(parts[shard, : out_rows - EDGE])
        tail = parts[shard, out_rows - EDGE : out_rows]
        if shard + 1 < shards:
            tail = tail + parts[shard + 1, out_rows:]
        rows.append(tail)
    series = jnp.concatenate(rows, axis=0).T
    real_part, imag_part = whitened(series, high_table[...], low_table[...], band[...])
    receivers_ref[:, :BINS] = real_part
    receivers_ref[:, BINS:] = imag_part

    for step in range(1, shards):
        piece_copy(step).wait_send()
        part_copy(step).wait_send()
    for step in range(shards):
        @pl.when((group != src) | (slot != step))
        def _():
            source_copy(step).wait_send()


def correlate_kernel(shards, group, receivers, sources, lags, index_ref, out, cross, lagged, sem):
    blk = lax.axis_index("blk")
    src = lax.axis_index("src")
    channels = receivers.shape[0]
    count = sources.shape[0]
    mine = lax.div(blk, shards) == src
    slot = lax.rem(blk, shards)

    def out_copy(row):
        local = lax.rem(row, shards) * 2 + lax.div(row, shards)
        return pltpu.make_async_copy(lagged.at[row], out.at[local], sem.at[row])

    @pl.loop(0, count // group)
    def _(step):
        for k in range(group):
            row = step * group + k
            src_re = sources[pl.ds(row, 1), :BINS]
            src_im = sources[pl.ds(row, 1), BINS:]
            rec_re = receivers[:, :BINS]
            rec_im = receivers[:, BINS:]
            cross[k * channels : (k + 1) * channels, :BINS] = (
                src_re * rec_re + src_im * rec_im
            ).astype(BF16)
            cross[k * channels : (k + 1) * channels, BINS:] = (
                src_re * rec_im - src_im * rec_re
            ).astype(BF16)
        product = dot(cross[...], lags[...])
        for k in range(group):
            row = step * group + k
            lagged[row] = product[k * channels : (k + 1) * channels].astype(BF16)

            @pl.when(mine & (lax.rem(row, shards) == slot))
            def _():
                channel = lax.broadcasted_iota(jnp.int32, (channels, LAGS), 0)
                own = channel == index_ref[0, lax.div(row, shards)]
                lagged[row] = jnp.where(own, 0.0, lagged[row].astype(F32)).astype(BF16)

            out_copy(row).start()

    @pl.loop(0, count)
    def _(row):
        out_copy(row).wait()


def local(raw_records, fir_taps, alive_mask, source_index):
    shards = lax.axis_size("src")
    channels, raw_count = raw_records.shape
    count = 2 * shards
    high_table, low_table = forward_tables()
    taps = jnp.pad(fir_taps, (0, LANES - TAPS)).reshape(1, LANES)
    vmem = pl.BlockSpec(memory_space=pltpu.VMEM)
    smem = pl.BlockSpec(memory_space=pltpu.SMEM)
    hbm = pl.BlockSpec(memory_space=pl.ANY)
    dma = pltpu.SemaphoreType.DMA
    receivers, sources = pl.pallas_call(
        functools.partial(gather_kernel, shards),
        out_shape=(
            jax.ShapeDtypeStruct((channels, NFFT), F32),
            jax.ShapeDtypeStruct((count, NFFT), F32),
        ),
        in_specs=[hbm, vmem, vmem, smem, hbm, hbm, hbm],
        out_specs=(vmem, vmem),
        scratch_shapes=[
            pltpu.VMEM((channels, raw_count), F32),
            pltpu.VMEM((S, NFFT), BF16),
            pltpu.VMEM((S, NFFT), BF16),
            pltpu.VMEM((BINS, BINS), BF16),
            pltpu.VMEM((shards, S // shards + EDGE, channels), F32),
            pltpu.VMEM((shards, 8, LANES), F32),
            pltpu.VMEM((8, LANES), F32),
            pltpu.VMEM((shards, 8, LANES), F32),
            dma((4,)),
            dma((shards,)),
            dma((shards,)),
            dma((shards,)),
            dma((shards,)),
            dma((shards,)),
            dma((shards,)),
        ],
        compiler_params=pltpu.CompilerParams(
            collective_id=0, has_side_effects=True, vmem_limit_bytes=32 << 20
        ),
        name="gather_whiten",
    )(
        raw_records,
        taps,
        alive_mask.reshape(1, channels),
        source_index,
        high_table,
        low_table,
        band_table(),
    )
    group = 4
    return pl.pallas_call(
        functools.partial(correlate_kernel, shards, group),
        out_shape=jax.ShapeDtypeStruct((count, channels, LAGS), BF16),
        in_specs=[vmem, vmem, vmem, smem],
        out_specs=hbm,
        scratch_shapes=[
            pltpu.VMEM((group * channels, NFFT), BF16),
            pltpu.VMEM((count, channels, LAGS), BF16),
            dma((count,)),
        ],
        compiler_params=pltpu.CompilerParams(vmem_limit_bytes=32 << 20),
        name="correlate",
    )(receivers, sources, lag_table(), source_index)


def solution(mesh):
    in_specs = (P("blk", "src"), P(), P("blk"), P("blk", None))
    out_specs = P("src", "blk", None)
    return jax.shard_map(local, mesh=mesh, in_specs=in_specs, out_specs=out_specs, check_vma=False)
```

```python
import functools
import math

import jax
import jax.numpy as jnp
import ml_dtypes
import numpy as np
from jax import lax
from jax.experimental import pallas as pl
from jax.experimental.pallas import tpu as pltpu
from jax.sharding import PartitionSpec as P

S = 512
NFFT = 1024
BINS = NFFT // 2
LAGS = 512
TAPS = 64
DEC = 20
HALF = 64
LANES = 128
EDGE = 8
MESH = pl.DeviceIdType.MESH
F32 = jnp.float32
BF16 = jnp.bfloat16


def split_np(table):
    high = table.astype(np.float32).astype(ml_dtypes.bfloat16)
    low = (table - high.astype(np.float64)).astype(ml_dtypes.bfloat16)
    return high, low


def forward_tables():
    phases = 2.0 * math.pi / NFFT * (np.outer(np.arange(S), np.arange(BINS)) % NFFT)
    return split_np(np.concatenate([np.cos(phases), -np.sin(phases)], axis=1))


def band_table():
    bins = np.arange(BINS)
    return (np.abs(bins[:, None] - bins[None, :]) <= HALF).astype(ml_dtypes.bfloat16)


def lag_table():
    bins = np.arange(BINS)
    shift = np.arange(LAGS) - LAGS // 2
    phases = 2.0 * math.pi / NFFT * (np.outer(bins, shift) % NFFT)
    weight = np.where(bins[:, None] == 0, 0.5, 1.0) / math.sqrt(BINS)
    table = np.concatenate([weight * np.cos(phases), -weight * np.sin(phases)], axis=0)
    return table.astype(np.float32).astype(ml_dtypes.bfloat16)


def split(value):
    high = value.astype(BF16)
    return high, (value - high.astype(F32)).astype(BF16)


def dot(a, b):
    return jnp.dot(a, b, preferred_element_type=F32)


def dot_nt(a, b):
    return lax.dot_general(a, b, (((1,), (1,)), ((), ())), preferred_element_type=F32)


def whitened(series, high_table, low_table, band):
    rows = series.shape[0]
    high, low = split(series)
    both = dot(jnp.concatenate([high, low], axis=0), high_table)
    spectrum = both[:rows] + both[rows:] + dot(high, low_table)
    real_part, imag_part = spectrum[:, :BINS], spectrum[:, BINS:]
    high, low = split(real_part * real_part + imag_part * imag_part)
    sums = dot(jnp.concatenate([high, low], axis=0), band)
    bins = lax.broadcasted_iota(jnp.int32, (1, BINS), 1)
    count = jnp.minimum(bins, HALF) + jnp.minimum(BINS - 1 - bins, HALF) + 1
    smooth = (sums[:rows] + sums[rows:]) / count.astype(F32)
    factor = lax.rsqrt(smooth + 1e-6)
    return real_part * factor, imag_part * factor


def tap_matrix(taps, raw_count, rows, edge_row):
    row = lax.broadcasted_iota(jnp.int32, (rows, LANES), 0)
    start = DEC * jnp.where(row < edge_row, row, row - rows)
    lane = lax.broadcasted_iota(jnp.int32, (rows, LANES), 1)
    padded = jnp.concatenate([taps, jnp.zeros((1, LANES - TAPS), F32)], axis=1)
    spread = jnp.broadcast_to(padded, (rows, LANES))
    turned = jnp.take_along_axis(spread, (lane - start) & (LANES - 1), axis=1)
    high, low = split(turned)
    high, low = high.astype(F32), low.astype(F32)
    highs, lows = [], []
    for first in range(0, raw_count, LANES):
        offset = lane + first - start
        inside = (offset >= 0) & (offset < TAPS)
        highs.append(jnp.where(inside, high, 0.0).astype(BF16))
        lows.append(jnp.where(inside, low, 0.0).astype(BF16))
    return jnp.concatenate(highs, axis=1), jnp.concatenate(lows, axis=1)


def gather_kernel(
    shards,
    raw_hbm,
    taps_hbm,
    alive_hbm,
    index_hbm,
    high_hbm,
    low_hbm,
    band_hbm,
    receivers_ref,
    sources_ref,
    raw,
    taps,
    alive,
    index,
    high_table,
    low_table,
    band,
    parts,
    pieces,
    packed,
    arrived,
    local_sem,
    piece_send,
    piece_recv,
    part_send,
    part_recv,
    source_send,
    source_recv,
):
    blk = lax.axis_index("blk")
    src = lax.axis_index("src")
    channels, raw_count = raw.shape
    out_rows = S // shards
    group = lax.div(blk, shards)
    slot = lax.rem(blk, shards)

    barrier = pltpu.get_barrier_semaphore()
    for step in range(1, shards):
        peer = lax.rem(src + step, shards)
        pl.semaphore_signal(barrier, inc=1, device_id=(blk, peer), device_id_type=MESH)
    for step in range(shards):
        @pl.when((group != src) | (slot != step))
        def _():
            pl.semaphore_signal(
                barrier, inc=1, device_id=(src * shards + step, group), device_id_type=MESH
            )

    loads = [
        pltpu.make_async_copy(source, target, local_sem.at[k])
        for k, (source, target) in enumerate(
            [
                (taps_hbm, taps),
                (raw_hbm, raw),
                (alive_hbm, alive),
                (index_hbm, index),
                (high_hbm, high_table),
                (low_hbm, low_table),
                (band_hbm, band),
            ]
        )
    ]
    for load in loads:
        load.start()

    loads[0].wait()
    tap_high, tap_low = tap_matrix(taps[...], raw_count, out_rows + EDGE, out_rows)
    for load in loads[1:4]:
        load.wait()
    raw_high, raw_low = split(raw[...])
    decimated = dot_nt(tap_high, raw_high) + dot_nt(tap_low, raw_high) + dot_nt(tap_high, raw_low)
    decimated = decimated * alive[...].astype(F32)
    parts[src] = decimated

    lane = lax.broadcasted_iota(jnp.int32, (8, channels), 1)
    row = lax.broadcasted_iota(jnp.int32, (8, channels), 0)
    chosen = jnp.where(row == 0, index[0, 0], jnp.where(row == 1, index[0, 1], -1))
    chooser = (lane == chosen).astype(F32).astype(BF16)
    padded = jnp.concatenate(
        [
            decimated[:out_rows],
            jnp.zeros((LANES - out_rows - EDGE, channels), F32),
            decimated[out_rows:],
        ],
        axis=0,
    )
    first, rest = split(padded)
    second, third = split(padded - first.astype(F32))
    pieces[src] = dot_nt(chooser, first) + dot_nt(chooser, second) + dot_nt(chooser, third)

    @pl.when(group != src)
    def _():
        pl.semaphore_wait(barrier, 2 * shards - 1)

    @pl.when(group == src)
    def _():
        pl.semaphore_wait(barrier, 2 * shards - 2)

    def piece_copy(step):
        return pltpu.make_async_remote_copy(
            src_ref=pieces.at[src],
            dst_ref=pieces.at[src],
            send_sem=piece_send.at[step],
            recv_sem=piece_recv.at[step],
            device_id=(blk, lax.rem(src + step, shards)),
            device_id_type=MESH,
        )

    def part_copy(step):
        return pltpu.make_async_remote_copy(
            src_ref=parts.at[src],
            dst_ref=parts.at[src],
            send_sem=part_send.at[step],
            recv_sem=part_recv.at[step],
            device_id=(blk, lax.rem(src + step, shards)),
            device_id_type=MESH,
        )

    def source_copy(step):
        return pltpu.make_async_remote_copy(
            src_ref=packed,
            dst_ref=arrived.at[slot],
            send_sem=source_send.at[step],
            recv_sem=source_recv.at[slot],
            device_id=(src * shards + step, group),
            device_id_type=MESH,
        )

    def source_arrival(step):
        return pltpu.make_async_remote_copy(
            src_ref=packed,
            dst_ref=arrived.at[step],
            send_sem=source_send.at[step],
            recv_sem=source_recv.at[step],
            device_id=(src * shards + step, group),
            device_id_type=MESH,
        )

    for step in range(1, shards):
        piece_copy(step).start()
    for step in range(1, shards):
        part_copy(step).start()

    for step in range(1, shards):
        piece_copy(step).wait_recv()
    lane = lax.broadcasted_iota(jnp.int32, (8, LANES), 1)
    for pair in range(shards // 2):
        after = pieces[2 * pair + 2] if 2 * pair + 2 < shards else jnp.zeros((8, LANES), F32)
        joined = pltpu.roll(pieces[2 * pair + 1], LANES // 2, 1) + jnp.where(
            lane < LANES // 2, pieces[2 * pair], after
        )
        packed[pair : pair + 1, :] = joined[0:1]
        packed[shards // 2 + pair : shards // 2 + pair + 1, :] = joined[1:2]

    for step in range(shards):
        me = (group == src) & (slot == step)

        @pl.when(me)
        def _():
            arrived[step] = packed[...]

        @pl.when(jnp.logical_not(me))
        def _():
            source_copy(step).start()

    for load in loads[4:]:
        load.wait()
    for step in range(shards):
        @pl.when((group != src) | (slot != step))
        def _():
            source_arrival(step).wait_recv()

    half = shards // 2
    sources = jnp.concatenate(
        [
            jnp.concatenate([arrived[:, v * half + pair, :] for pair in range(half)], axis=1)
            for v in range(2)
        ],
        axis=0,
    )
    real_part, imag_part = whitened(sources, high_table[...], low_table[...], band[...])
    sources_ref[:, :BINS] = real_part
    sources_ref[:, BINS:] = imag_part

    for step in range(1, shards):
        part_copy(step).wait_recv()
    rows = []
    for shard in range(shards):
        rows.append(parts[shard, : out_rows - EDGE])
        tail = parts[shard, out_rows - EDGE : out_rows]
        if shard + 1 < shards:
            tail = tail + parts[shard + 1, out_rows:]
        rows.append(tail)
    series = jnp.concatenate(rows, axis=0).T
    real_part, imag_part = whitened(series, high_table[...], low_table[...], band[...])
    receivers_ref[:, :BINS] = real_part
    receivers_ref[:, BINS:] = imag_part

    for step in range(1, shards):
        piece_copy(step).wait_send()
        part_copy(step).wait_send()
    for step in range(shards):
        @pl.when((group != src) | (slot != step))
        def _():
            source_copy(step).wait_send()


def correlate_kernel(shards, group, receivers, sources, lags, index_ref, out, cross, lagged, sem):
    blk = lax.axis_index("blk")
    src = lax.axis_index("src")
    channels = receivers.shape[0]
    count = sources.shape[0]
    mine = lax.div(blk, shards) == src
    slot = lax.rem(blk, shards)

    def out_copy(row):
        local = lax.rem(row, shards) * 2 + lax.div(row, shards)
        return pltpu.make_async_copy(lagged.at[row], out.at[local], sem.at[row])

    @pl.loop(0, count // group)
    def _(step):
        for k in range(group):
            row = step * group + k
            src_re = sources[pl.ds(row, 1), :BINS]
            src_im = sources[pl.ds(row, 1), BINS:]
            rec_re = receivers[:, :BINS]
            rec_im = receivers[:, BINS:]
            cross[k * channels : (k + 1) * channels, :BINS] = (
                src_re * rec_re + src_im * rec_im
            ).astype(BF16)
            cross[k * channels : (k + 1) * channels, BINS:] = (
                src_re * rec_im - src_im * rec_re
            ).astype(BF16)
        product = dot(cross[...], lags[...])
        for k in range(group):
            row = step * group + k
            lagged[row] = product[k * channels : (k + 1) * channels].astype(BF16)

            @pl.when(mine & (lax.rem(row, shards) == slot))
            def _():
                channel = lax.broadcasted_iota(jnp.int32, (channels, LAGS), 0)
                own = channel == index_ref[0, lax.div(row, shards)]
                lagged[row] = jnp.where(own, 0.0, lagged[row].astype(F32)).astype(BF16)

            out_copy(row).start()

    @pl.loop(0, count)
    def _(row):
        out_copy(row).wait()


def local(raw_records, fir_taps, alive_mask, source_index):
    shards = lax.axis_size("src")
    channels, raw_count = raw_records.shape
    count = 2 * shards
    high_table, low_table = forward_tables()
    vmem = pl.BlockSpec(memory_space=pltpu.VMEM)
    smem = pl.BlockSpec(memory_space=pltpu.SMEM)
    hbm = pl.BlockSpec(memory_space=pltpu.HBM)
    dma = pltpu.SemaphoreType.DMA
    receivers, sources = pl.pallas_call(
        functools.partial(gather_kernel, shards),
        out_shape=(
            jax.ShapeDtypeStruct((channels, NFFT), F32),
            jax.ShapeDtypeStruct((count, NFFT), F32),
        ),
        in_specs=[hbm] * 7,
        out_specs=(vmem, vmem),
        scratch_shapes=[
            pltpu.VMEM((channels, raw_count), F32),
            pltpu.VMEM((1, TAPS), F32),
            pltpu.VMEM((1, channels), jnp.int32),
            pltpu.SMEM((1, 2), jnp.int32),
            pltpu.VMEM((S, NFFT), BF16),
            pltpu.VMEM((S, NFFT), BF16),
            pltpu.VMEM((BINS, BINS), BF16),
            pltpu.VMEM((shards, S // shards + EDGE, channels), F32),
            pltpu.VMEM((shards, 8, LANES), F32),
            pltpu.VMEM((8, LANES), F32),
            pltpu.VMEM((shards, 8, LANES), F32),
            dma((7,)),
            dma((shards,)),
            dma((shards,)),
            dma((shards,)),
            dma((shards,)),
            dma((shards,)),
            dma((shards,)),
        ],
        compiler_params=pltpu.CompilerParams(
            collective_id=0, has_side_effects=True, vmem_limit_bytes=60 << 20
        ),
        name="gather_whiten",
    )(
        raw_records,
        fir_taps.reshape(1, TAPS),
        alive_mask.reshape(1, channels),
        source_index,
        high_table,
        low_table,
        band_table(),
    )
    group = 4
    return pl.pallas_call(
        functools.partial(correlate_kernel, shards, group),
        out_shape=jax.ShapeDtypeStruct((count, channels, LAGS), BF16),
        in_specs=[vmem, vmem, vmem, smem],
        out_specs=hbm,
        scratch_shapes=[
            pltpu.VMEM((group * channels, NFFT), BF16),
            pltpu.VMEM((count, channels, LAGS), BF16),
            dma((count,)),
        ],
        compiler_params=pltpu.CompilerParams(vmem_limit_bytes=60 << 20),
        name="correlate",
    )(receivers, sources, lag_table(), source_index)


def solution(mesh):
    in_specs = (P("blk", "src"), P(), P("blk"), P("blk", None))
    out_specs = P("src", "blk", None)
    return jax.shard_map(local, mesh=mesh, in_specs=in_specs, out_specs=out_specs, check_vma=False)
```

```python
import functools
import math

import jax
import jax.numpy as jnp
import ml_dtypes
import numpy as np
from jax import lax
from jax.experimental import pallas as pl
from jax.experimental.pallas import tpu as pltpu
from jax.sharding import PartitionSpec as P

S = 512
NFFT = 1024
BINS = NFFT // 2
LAGS = 512
TAPS = 64
DEC = 20
HALF = 64
LANES = 128
EDGE = 8
MESH = pl.DeviceIdType.MESH
F32 = jnp.float32
BF16 = jnp.bfloat16


def split_np(table):
    high = table.astype(np.float32).astype(ml_dtypes.bfloat16)
    low = (table - high.astype(np.float64)).astype(ml_dtypes.bfloat16)
    return high, low


def forward_tables():
    phases = 2.0 * math.pi / NFFT * (np.outer(np.arange(S), np.arange(BINS)) % NFFT)
    return split_np(np.concatenate([np.cos(phases), -np.sin(phases)], axis=1))


def band_table():
    bins = np.arange(BINS)
    return (np.abs(bins[:, None] - bins[None, :]) <= HALF).astype(ml_dtypes.bfloat16)


def lag_table():
    bins = np.arange(BINS)
    shift = np.arange(LAGS) - LAGS // 2
    phases = 2.0 * math.pi / NFFT * (np.outer(bins, shift) % NFFT)
    weight = np.where(bins[:, None] == 0, 0.5, 1.0) / math.sqrt(BINS)
    table = np.concatenate([weight * np.cos(phases), -weight * np.sin(phases)], axis=0)
    return table.astype(np.float32).astype(ml_dtypes.bfloat16)


def split(value):
    high = value.astype(BF16)
    return high, (value - high.astype(F32)).astype(BF16)


def dot(a, b):
    return jnp.dot(a, b, preferred_element_type=F32)


def dot_nt(a, b):
    return lax.dot_general(a, b, (((1,), (1,)), ((), ())), preferred_element_type=F32)


def whitened(series, high_table, low_table, band):
    rows = series.shape[0]
    high, low = split(series)
    both = dot(jnp.concatenate([high, low], axis=0), high_table)
    spectrum = both[:rows] + both[rows:] + dot(high, low_table)
    real_part, imag_part = spectrum[:, :BINS], spectrum[:, BINS:]
    high, low = split(real_part * real_part + imag_part * imag_part)
    sums = dot(jnp.concatenate([high, low], axis=0), band)
    bins = lax.broadcasted_iota(jnp.int32, (1, BINS), 1)
    count = jnp.minimum(bins, HALF) + jnp.minimum(BINS - 1 - bins, HALF) + 1
    smooth = (sums[:rows] + sums[rows:]) / count.astype(F32)
    factor = lax.rsqrt(smooth + 1e-6)
    return real_part * factor, imag_part * factor


def tap_matrix(taps, raw_count, rows, edge_row):
    row = lax.broadcasted_iota(jnp.int32, (rows, LANES), 0)
    start = DEC * jnp.where(row < edge_row, row, row - rows)
    lane = lax.broadcasted_iota(jnp.int32, (rows, LANES), 1)
    padded = jnp.concatenate([taps, jnp.zeros((1, LANES - TAPS), F32)], axis=1)
    spread = jnp.broadcast_to(padded, (rows, LANES))
    turned = jnp.take_along_axis(spread, (lane - start) & (LANES - 1), axis=1)
    high, low = split(turned)
    high, low = high.astype(F32), low.astype(F32)
    highs, lows = [], []
    for first in range(0, raw_count, LANES):
        offset = lane + first - start
        inside = (offset >= 0) & (offset < TAPS)
        highs.append(jnp.where(inside, high, 0.0).astype(BF16))
        lows.append(jnp.where(inside, low, 0.0).astype(BF16))
    return jnp.concatenate(highs, axis=1), jnp.concatenate(lows, axis=1)


def gather_kernel(
    shards,
    blocks,
    raw_hbm,
    taps_hbm,
    alive_hbm,
    index_hbm,
    high_hbm,
    low_hbm,
    band_hbm,
    receivers_ref,
    sources_ref,
    raw,
    taps,
    alive,
    index,
    high_table,
    low_table,
    band,
    parts,
    pieces,
    packed,
    arrived,
    local_sem,
    piece_send,
    piece_recv,
    part_send,
    part_recv,
    source_send,
    source_recv,
):
    blk = lax.axis_index("blk")
    src = lax.axis_index("src")
    channels, raw_count = raw.shape
    out_rows = S // shards
    half = shards // 2
    group = lax.div(blk, shards)
    slot = lax.rem(blk, shards)
    leads = src == group

    barrier = pltpu.get_barrier_semaphore()
    for step in range(shards):
        @pl.when(jnp.logical_not(leads) | (slot != step))
        def _():
            pl.semaphore_signal(
                barrier, inc=1, device_id=(src * shards + step, src), device_id_type=MESH
            )
    for step in range(1, shards):
        peer = lax.rem(src + step, shards)
        pl.semaphore_signal(barrier, inc=1, device_id=(blk, peer), device_id_type=MESH)

    loads = [
        pltpu.make_async_copy(source, target, local_sem.at[k])
        for k, (source, target) in enumerate(
            [
                (taps_hbm, taps),
                (raw_hbm, raw),
                (alive_hbm, alive),
                (index_hbm, index),
                (high_hbm, high_table),
                (low_hbm, low_table),
                (band_hbm, band),
            ]
        )
    ]
    for load in loads:
        load.start()

    loads[0].wait()
    tap_high, tap_low = tap_matrix(taps[...], raw_count, out_rows + EDGE, out_rows)
    for load in loads[1:4]:
        load.wait()
    raw_high, raw_low = split(raw[...])
    decimated = dot_nt(tap_high, raw_high) + dot_nt(tap_low, raw_high) + dot_nt(tap_high, raw_low)
    decimated = decimated * alive[...].astype(F32)
    parts[src] = decimated

    lane = lax.broadcasted_iota(jnp.int32, (8, channels), 1)
    row = lax.broadcasted_iota(jnp.int32, (8, channels), 0)
    chosen = jnp.where(row == 0, index[0, 0], jnp.where(row == 1, index[0, 1], -1))
    chooser = (lane == chosen).astype(F32).astype(BF16)
    padded = jnp.concatenate(
        [
            decimated[:out_rows],
            jnp.zeros((LANES - out_rows - EDGE, channels), F32),
            decimated[out_rows:],
        ],
        axis=0,
    )
    first, rest = split(padded)
    second, third = split(padded - first.astype(F32))
    pieces[src] = dot_nt(chooser, first) + dot_nt(chooser, second) + dot_nt(chooser, third)

    def piece_copy(shard):
        return pltpu.make_async_remote_copy(
            src_ref=pieces.at[shard],
            dst_ref=pieces.at[shard],
            send_sem=piece_send,
            recv_sem=piece_recv.at[shard],
            device_id=(blk, group),
            device_id_type=MESH,
        )

    def part_copy(step):
        return pltpu.make_async_remote_copy(
            src_ref=parts.at[src],
            dst_ref=parts.at[src],
            send_sem=part_send.at[step],
            recv_sem=part_recv.at[step],
            device_id=(blk, lax.rem(src + step, shards)),
            device_id_type=MESH,
        )

    def source_copy(step):
        target = lax.rem(lax.div(step, 4), 2) * (blocks // 2) + lax.div(step, 8) * 4 + lax.rem(step, 4)
        return target, pltpu.make_async_remote_copy(
            src_ref=packed,
            dst_ref=arrived.at[slot],
            send_sem=source_send.at[step],
            recv_sem=source_recv.at[slot],
            device_id=(target, group),
            device_id_type=MESH,
        )

    @pl.when(jnp.logical_not(leads))
    def _():
        pl.semaphore_wait(barrier, shards - 1)
        piece_copy(src).start()

    @pl.when(leads)
    def _():
        pl.semaphore_wait(barrier, shards - 1 + blocks - 1)

    for step in range(1, shards):
        part_copy(step).start()

    @pl.when(leads)
    def _():
        for step in range(1, shards):
            shard = lax.rem(src + step, shards)
            pltpu.make_async_copy(pieces.at[shard], pieces.at[shard], piece_recv.at[shard]).wait()
        lane = lax.broadcasted_iota(jnp.int32, (8, LANES), 1)
        for pair in range(half):
            after = pieces[2 * pair + 2] if 2 * pair + 2 < shards else jnp.zeros((8, LANES), F32)
            joined = pltpu.roll(pieces[2 * pair + 1], LANES // 2, 1) + jnp.where(
                lane < LANES // 2, pieces[2 * pair], after
            )
            packed[pair : pair + 1, :] = joined[0:1]
            packed[half + pair : half + pair + 1, :] = joined[1:2]

        @pl.loop(0, blocks)
        def _(step):
            target, copy = source_copy(step)

            @pl.when(target != blk)
            def _():
                copy.start()

        arrived[slot] = packed[...]

    for load in loads[4:]:
        load.wait()
    for step in range(1, shards):
        part_copy(step).wait_recv()
    rows = []
    for shard in range(shards):
        rows.append(parts[shard, : out_rows - EDGE])
        tail = parts[shard, out_rows - EDGE : out_rows]
        if shard + 1 < shards:
            tail = tail + parts[shard + 1, out_rows:]
        rows.append(tail)
    series = jnp.concatenate(rows, axis=0).T
    real_part, imag_part = whitened(series, high_table[...], low_table[...], band[...])
    receivers_ref[:, :BINS] = real_part
    receivers_ref[:, BINS:] = imag_part

    for step in range(shards):
        @pl.when(jnp.logical_not(leads) | (slot != step))
        def _():
            pltpu.make_async_copy(arrived.at[step], arrived.at[step], source_recv.at[step]).wait()
    sources = jnp.concatenate(
        [
            jnp.concatenate([arrived[:, v * half + pair, :] for pair in range(half)], axis=1)
            for v in range(2)
        ],
        axis=0,
    )
    real_part, imag_part = whitened(sources, high_table[...], low_table[...], band[...])
    sources_ref[:, :BINS] = real_part
    sources_ref[:, BINS:] = imag_part

    for step in range(1, shards):
        part_copy(step).wait_send()

    @pl.when(jnp.logical_not(leads))
    def _():
        piece_copy(src).wait_send()

    @pl.when(leads)
    def _():
        @pl.loop(0, blocks)
        def _(step):
            target, copy = source_copy(step)

            @pl.when(target != blk)
            def _():
                copy.wait_send()


def correlate_kernel(shards, group, receivers, sources, lags, index_ref, out, cross, lagged, sem):
    blk = lax.axis_index("blk")
    src = lax.axis_index("src")
    channels = receivers.shape[0]
    count = sources.shape[0]
    mine = lax.div(blk, shards) == src
    slot = lax.rem(blk, shards)

    def out_copy(row):
        local = lax.rem(row, shards) * 2 + lax.div(row, shards)
        return pltpu.make_async_copy(lagged.at[row], out.at[local], sem.at[row])

    def form(step):
        for k in range(group):
            row = step * group + k
            rows = pl.ds((step % 2 * group + k) * channels, channels)
            src_re, src_im = sources[row : row + 1, :BINS], sources[row : row + 1, BINS:]
            rec_re, rec_im = receivers[:, :BINS], receivers[:, BINS:]
            cross[rows, :BINS] = (src_re * rec_re + src_im * rec_im).astype(BF16)
            cross[rows, BINS:] = (src_re * rec_im - src_im * rec_re).astype(BF16)

    channel = lax.broadcasted_iota(jnp.int32, (channels, 1), 0)
    form(0)
    for step in range(count // group):
        if step + 1 < count // group:
            form(step + 1)
        size = group * channels
        product = dot(cross[pl.ds(step % 2 * size, size)], lags[...])
        for k in range(group):
            row = step * group + k
            chosen = jnp.where(mine & (row % shards == slot), index_ref[0, row // shards], -1)
            kept = jnp.where(channel == chosen, 0.0, product[k * channels : (k + 1) * channels])
            lagged[row] = kept.astype(BF16)
            out_copy(row).start()

    @pl.loop(0, count)
    def _(row):
        out_copy(row).wait()


def local(raw_records, fir_taps, alive_mask, source_index):
    shards = lax.axis_size("src")
    blocks = lax.axis_size("blk")
    channels, raw_count = raw_records.shape
    count = 2 * shards
    high_table, low_table = forward_tables()
    vmem = pl.BlockSpec(memory_space=pltpu.VMEM)
    smem = pl.BlockSpec(memory_space=pltpu.SMEM)
    hbm = pl.BlockSpec(memory_space=pltpu.HBM)
    dma = pltpu.SemaphoreType.DMA
    receivers, sources = pl.pallas_call(
        functools.partial(gather_kernel, shards, blocks),
        out_shape=(
            jax.ShapeDtypeStruct((channels, NFFT), F32),
            jax.ShapeDtypeStruct((count, NFFT), F32),
        ),
        in_specs=[hbm] * 7,
        out_specs=(vmem, vmem),
        scratch_shapes=[
            pltpu.VMEM((channels, raw_count), F32),
            pltpu.VMEM((1, TAPS), F32),
            pltpu.VMEM((1, channels), jnp.int32),
            pltpu.SMEM((1, 2), jnp.int32),
            pltpu.VMEM((S, NFFT), BF16),
            pltpu.VMEM((S, NFFT), BF16),
            pltpu.VMEM((BINS, BINS), BF16),
            pltpu.VMEM((shards, S // shards + EDGE, channels), F32),
            pltpu.VMEM((shards, 8, LANES), F32),
            pltpu.VMEM((8, LANES), F32),
            pltpu.VMEM((shards, 8, LANES), F32),
            dma((7,)),
            dma,
            dma((shards,)),
            dma((shards,)),
            dma((shards,)),
            dma((blocks,)),
            dma((shards,)),
        ],
        compiler_params=pltpu.CompilerParams(
            collective_id=0, has_side_effects=True, vmem_limit_bytes=24 << 20
        ),
        name="gather_whiten",
    )(
        *(
            pltpu.with_memory_space_constraint(jnp.asarray(operand), pltpu.HBM)
            for operand in (
                raw_records,
                fir_taps.reshape(1, TAPS),
                alive_mask.reshape(1, channels),
                source_index,
                high_table,
                low_table,
                band_table(),
            )
        )
    )
    group = 2
    return pl.pallas_call(
        functools.partial(correlate_kernel, shards, group),
        out_shape=jax.ShapeDtypeStruct((count, channels, LAGS), BF16),
        in_specs=[vmem, vmem, vmem, smem],
        out_specs=hbm,
        scratch_shapes=[
            pltpu.VMEM((2 * group * channels, NFFT), BF16),
            pltpu.VMEM((count, channels, LAGS), BF16),
            dma((count,)),
        ],
        compiler_params=pltpu.CompilerParams(vmem_limit_bytes=24 << 20),
        name="correlate",
    )(receivers, sources, lag_table(), source_index)


def solution(mesh):
    in_specs = (P("blk", "src"), P(), P("blk"), P("blk", None))
    out_specs = P("src", "blk", None)
    return jax.shard_map(local, mesh=mesh, in_specs=in_specs, out_specs=out_specs, check_vma=False)
```

```python
import functools
import math

import jax
import jax.numpy as jnp
import ml_dtypes
import numpy as np
from jax import lax
from jax.experimental import pallas as pl
from jax.experimental.pallas import tpu as pltpu
from jax.sharding import PartitionSpec as P

S = 512
NFFT = 1024
BINS = NFFT // 2
LAGS = 512
TAPS = 64
DEC = 20
HALF = 64
LANES = 128
EDGE = 8
MESH = pl.DeviceIdType.MESH
F32 = jnp.float32
BF16 = jnp.bfloat16


def split_np(table):
    high = table.astype(np.float32).astype(ml_dtypes.bfloat16)
    low = (table - high.astype(np.float64)).astype(ml_dtypes.bfloat16)
    return high, low


def forward_tables():
    phases = 2.0 * math.pi / NFFT * (np.outer(np.arange(S), np.arange(BINS)) % NFFT)
    return split_np(np.concatenate([np.cos(phases), -np.sin(phases)], axis=1))


def band_table():
    bins = np.arange(BINS)
    return (np.abs(bins[:, None] - bins[None, :]) <= HALF).astype(ml_dtypes.bfloat16)


def lag_table():
    bins = np.arange(BINS)
    shift = np.arange(LAGS) - LAGS // 2
    phases = 2.0 * math.pi / NFFT * (np.outer(bins, shift) % NFFT)
    weight = np.where(bins[:, None] == 0, 0.5, 1.0) / math.sqrt(BINS)
    table = np.concatenate([weight * np.cos(phases), -weight * np.sin(phases)], axis=0)
    return table.astype(np.float32).astype(ml_dtypes.bfloat16)


def split(value):
    high = value.astype(BF16)
    return high, (value - high.astype(F32)).astype(BF16)


def dot(a, b):
    return jnp.dot(a, b, preferred_element_type=F32)


def dot_nt(a, b):
    return lax.dot_general(a, b, (((1,), (1,)), ((), ())), preferred_element_type=F32)


def whitened(series, high_table, low_table, band):
    rows = series.shape[0]
    high, low = split(series)
    both = dot(jnp.concatenate([high, low], axis=0), high_table)
    spectrum = both[:rows] + both[rows:] + dot(high, low_table)
    real_part, imag_part = spectrum[:, :BINS], spectrum[:, BINS:]
    high, low = split(real_part * real_part + imag_part * imag_part)
    sums = dot(jnp.concatenate([high, low], axis=0), band)
    bins = lax.broadcasted_iota(jnp.int32, (1, BINS), 1)
    count = jnp.minimum(bins, HALF) + jnp.minimum(BINS - 1 - bins, HALF) + 1
    smooth = (sums[:rows] + sums[rows:]) / count.astype(F32)
    factor = lax.rsqrt(smooth + 1e-6)
    return real_part * factor, imag_part * factor


def tap_matrix(taps, raw_count, rows, edge_row):
    row = lax.broadcasted_iota(jnp.int32, (rows, LANES), 0)
    start = DEC * jnp.where(row < edge_row, row, row - rows)
    lane = lax.broadcasted_iota(jnp.int32, (rows, LANES), 1)
    padded = jnp.concatenate([taps, jnp.zeros((1, LANES - TAPS), F32)], axis=1)
    spread = jnp.broadcast_to(padded, (rows, LANES))
    turned = jnp.take_along_axis(spread, (lane - start) & (LANES - 1), axis=1)
    high, low = split(turned)
    high, low = high.astype(F32), low.astype(F32)
    highs, lows = [], []
    for first in range(0, raw_count, LANES):
        offset = lane + first - start
        inside = (offset >= 0) & (offset < TAPS)
        highs.append(jnp.where(inside, high, 0.0).astype(BF16))
        lows.append(jnp.where(inside, low, 0.0).astype(BF16))
    return jnp.concatenate(highs, axis=1), jnp.concatenate(lows, axis=1)


def gather_kernel(
    shards,
    blocks,
    raw_hbm,
    taps_hbm,
    alive_hbm,
    index_hbm,
    high_hbm,
    low_hbm,
    band_hbm,
    receivers_ref,
    sources_ref,
    raw,
    taps,
    alive,
    index,
    high_table,
    low_table,
    band,
    parts,
    pieces,
    packed,
    arrived,
    local_sem,
    piece_send,
    piece_recv,
    part_send,
    part_recv,
    source_send,
    source_recv,
):
    blk = lax.axis_index("blk")
    src = lax.axis_index("src")
    channels, raw_count = raw.shape
    out_rows = S // shards
    half = shards // 2
    chip = lax.div(src, 2)
    core = lax.rem(src, 2)
    sibling = 2 * chip + 1 - core
    group = lax.div(blk, shards)
    slot = lax.rem(blk, shards)
    leads = src == group

    barrier = pltpu.get_barrier_semaphore()
    for step in range(shards):
        @pl.when(jnp.logical_not(leads) | (slot != step))
        def _():
            pl.semaphore_signal(
                barrier, inc=1, device_id=(src * shards + step, src), device_id_type=MESH
            )
    for step in range(1, shards):
        peer = lax.rem(src + step, shards)
        pl.semaphore_signal(barrier, inc=1, device_id=(blk, peer), device_id_type=MESH)

    loads = [
        pltpu.make_async_copy(source, target, local_sem.at[k])
        for k, (source, target) in enumerate(
            [
                (taps_hbm, taps),
                (raw_hbm, raw),
                (alive_hbm, alive),
                (index_hbm, index),
                (high_hbm, high_table),
                (low_hbm, low_table),
                (band_hbm, band),
            ]
        )
    ]
    for load in loads:
        load.start()

    loads[0].wait()
    tap_high, tap_low = tap_matrix(taps[...], raw_count, out_rows + EDGE, out_rows)
    for load in loads[1:4]:
        load.wait()
    raw_high, raw_low = split(raw[...])
    decimated = dot_nt(tap_high, raw_high) + dot_nt(tap_low, raw_high) + dot_nt(tap_high, raw_low)
    decimated = decimated * alive[...].astype(F32)
    parts[src] = decimated

    lane = lax.broadcasted_iota(jnp.int32, (8, channels), 1)
    row = lax.broadcasted_iota(jnp.int32, (8, channels), 0)
    chosen = jnp.where(row == 0, index[0, 0], jnp.where(row == 1, index[0, 1], -1))
    chooser = (lane == chosen).astype(F32).astype(BF16)
    padded = jnp.concatenate(
        [
            decimated[:out_rows],
            jnp.zeros((LANES - out_rows - EDGE, channels), F32),
            decimated[out_rows:],
        ],
        axis=0,
    )
    first, rest = split(padded)
    second, third = split(padded - first.astype(F32))
    pieces[src] = dot_nt(chooser, first) + dot_nt(chooser, second) + dot_nt(chooser, third)

    def piece_copy(shard):
        return pltpu.make_async_remote_copy(
            src_ref=pieces.at[shard],
            dst_ref=pieces.at[shard],
            send_sem=piece_send,
            recv_sem=piece_recv.at[shard],
            device_id=(blk, group),
            device_id_type=MESH,
        )

    def part_copy(shard, sem, peer):
        return pltpu.make_async_remote_copy(
            src_ref=parts.at[shard],
            dst_ref=parts.at[shard],
            send_sem=part_send.at[sem],
            recv_sem=part_recv.at[shard],
            device_id=(blk, peer),
            device_id_type=MESH,
        )

    def own_part(step):
        other = lax.rem(chip + step, half)
        heard = jnp.where(other == lax.div(group, 2), 1 - lax.rem(group, 2), core)
        return part_copy(src, step, sibling if step == 0 else 2 * other + heard)

    def handed_part(step):
        of_core = step % 2
        shard = 2 * lax.rem(chip + 1 + step // 2, half) + of_core
        hands = jnp.logical_not(leads) & ((of_core == core) | (sibling == group))
        return shard, hands, part_copy(shard, half + step, sibling)

    def await_part(shard):
        pltpu.make_async_copy(parts.at[shard], parts.at[shard], part_recv.at[shard]).wait()

    def source_copy(step):
        target = lax.rem(lax.div(step, 4), 2) * (blocks // 2) + lax.div(step, 8) * 4 + lax.rem(step, 4)
        return target, pltpu.make_async_remote_copy(
            src_ref=packed,
            dst_ref=arrived.at[slot],
            send_sem=source_send.at[step],
            recv_sem=source_recv.at[slot],
            device_id=(target, group),
            device_id_type=MESH,
        )

    @pl.when(jnp.logical_not(leads))
    def _():
        pl.semaphore_wait(barrier, shards - 1)
        piece_copy(src).start()

    @pl.when(leads)
    def _():
        pl.semaphore_wait(barrier, shards - 1 + blocks - 1)

    for step in range(half):
        own_part(step).start()

    @pl.when(leads)
    def _():
        for step in range(1, shards):
            shard = lax.rem(src + step, shards)
            pltpu.make_async_copy(pieces.at[shard], pieces.at[shard], piece_recv.at[shard]).wait()
        lane = lax.broadcasted_iota(jnp.int32, (8, LANES), 1)
        for pair in range(half):
            after = pieces[2 * pair + 2] if 2 * pair + 2 < shards else jnp.zeros((8, LANES), F32)
            joined = pltpu.roll(pieces[2 * pair + 1], LANES // 2, 1) + jnp.where(
                lane < LANES // 2, pieces[2 * pair], after
            )
            packed[pair : pair + 1, :] = joined[0:1]
            packed[half + pair : half + pair + 1, :] = joined[1:2]

        @pl.loop(0, blocks)
        def _(step):
            target, copy = source_copy(step)

            @pl.when(target != blk)
            def _():
                copy.start()

        arrived[slot] = packed[...]

    for step in range(shards - 2):
        shard, hands, copy = handed_part(step)

        @pl.when(hands)
        def _():
            await_part(shard)
            copy.start()

    for load in loads[4:]:
        load.wait()
    await_part(sibling)
    for step in range(shards - 2):
        shard, hands, copy = handed_part(step)

        @pl.when(jnp.logical_not(hands))
        def _():
            await_part(shard)

    rows = []
    for shard in range(shards):
        rows.append(parts[shard, : out_rows - EDGE])
        tail = parts[shard, out_rows - EDGE : out_rows]
        if shard + 1 < shards:
            tail = tail + parts[shard + 1, out_rows:]
        rows.append(tail)
    series = jnp.concatenate(rows, axis=0).T
    real_part, imag_part = whitened(series, high_table[...], low_table[...], band[...])
    receivers_ref[:, :BINS] = real_part
    receivers_ref[:, BINS:] = imag_part

    for step in range(shards):
        @pl.when(jnp.logical_not(leads) | (slot != step))
        def _():
            pltpu.make_async_copy(arrived.at[step], arrived.at[step], source_recv.at[step]).wait()
    sources = jnp.concatenate(
        [
            jnp.concatenate([arrived[:, v * half + pair, :] for pair in range(half)], axis=1)
            for v in range(2)
        ],
        axis=0,
    )
    real_part, imag_part = whitened(sources, high_table[...], low_table[...], band[...])
    sources_ref[:, :BINS] = real_part
    sources_ref[:, BINS:] = imag_part

    for step in range(half):
        own_part(step).wait_send()
    for step in range(shards - 2):
        shard, hands, copy = handed_part(step)

        @pl.when(hands)
        def _():
            copy.wait_send()


    @pl.when(jnp.logical_not(leads))
    def _():
        piece_copy(src).wait_send()

    @pl.when(leads)
    def _():
        @pl.loop(0, blocks)
        def _(step):
            target, copy = source_copy(step)

            @pl.when(target != blk)
            def _():
                copy.wait_send()


def correlate_kernel(shards, group, receivers, sources, lags, index_ref, out, cross, lagged, sem):
    blk = lax.axis_index("blk")
    src = lax.axis_index("src")
    channels = receivers.shape[0]
    count = sources.shape[0]
    mine = lax.div(blk, shards) == src
    slot = lax.rem(blk, shards)

    def out_copy(row):
        local = lax.rem(row, shards) * 2 + lax.div(row, shards)
        return pltpu.make_async_copy(lagged.at[row], out.at[local], sem.at[row])

    def form(step):
        for k in range(group):
            row = step * group + k
            rows = pl.ds((step % 2 * group + k) * channels, channels)
            src_re, src_im = sources[row : row + 1, :BINS], sources[row : row + 1, BINS:]
            rec_re, rec_im = receivers[:, :BINS], receivers[:, BINS:]
            cross[rows, :BINS] = (src_re * rec_re + src_im * rec_im).astype(BF16)
            cross[rows, BINS:] = (src_re * rec_im - src_im * rec_re).astype(BF16)

    channel = lax.broadcasted_iota(jnp.int32, (channels, 1), 0)
    form(0)
    for step in range(count // group):
        if step + 1 < count // group:
            form(step + 1)
        size = group * channels
        product = dot(cross[pl.ds(step % 2 * size, size)], lags[...])
        for k in range(group):
            row = step * group + k
            chosen = jnp.where(mine & (row % shards == slot), index_ref[0, row // shards], -1)
            kept = jnp.where(channel == chosen, 0.0, product[k * channels : (k + 1) * channels])
            lagged[row] = kept.astype(BF16)
            out_copy(row).start()

    @pl.loop(0, count)
    def _(row):
        out_copy(row).wait()


def local(raw_records, fir_taps, alive_mask, source_index):
    shards = lax.axis_size("src")
    blocks = lax.axis_size("blk")
    channels, raw_count = raw_records.shape
    count = 2 * shards
    high_table, low_table = forward_tables()
    vmem = pl.BlockSpec(memory_space=pltpu.VMEM)
    smem = pl.BlockSpec(memory_space=pltpu.SMEM)
    hbm = pl.BlockSpec(memory_space=pltpu.HBM)
    dma = pltpu.SemaphoreType.DMA
    receivers, sources = pl.pallas_call(
        functools.partial(gather_kernel, shards, blocks),
        out_shape=(
            jax.ShapeDtypeStruct((channels, NFFT), F32),
            jax.ShapeDtypeStruct((count, NFFT), F32),
        ),
        in_specs=[hbm] * 7,
        out_specs=(vmem, vmem),
        scratch_shapes=[
            pltpu.VMEM((channels, raw_count), F32),
            pltpu.VMEM((1, TAPS), F32),
            pltpu.VMEM((1, channels), jnp.int32),
            pltpu.SMEM((1, 2), jnp.int32),
            pltpu.VMEM((S, NFFT), BF16),
            pltpu.VMEM((S, NFFT), BF16),
            pltpu.VMEM((BINS, BINS), BF16),
            pltpu.VMEM((shards, S // shards + EDGE, channels), F32),
            pltpu.VMEM((shards, 8, LANES), F32),
            pltpu.VMEM((8, LANES), F32),
            pltpu.VMEM((shards, 8, LANES), F32),
            dma((7,)),
            dma,
            dma((shards,)),
            dma((shards // 2 + shards - 2,)),
            dma((shards,)),
            dma((blocks,)),
            dma((shards,)),
        ],
        compiler_params=pltpu.CompilerParams(
            collective_id=0, has_side_effects=True, vmem_limit_bytes=24 << 20
        ),
        name="gather_whiten",
    )(
        *(
            pltpu.with_memory_space_constraint(jnp.asarray(operand), pltpu.HBM)
            for operand in (
                raw_records,
                fir_taps.reshape(1, TAPS),
                alive_mask.reshape(1, channels),
                source_index,
                high_table,
                low_table,
                band_table(),
            )
        )
    )
    group = 2
    return pl.pallas_call(
        functools.partial(correlate_kernel, shards, group),
        out_shape=jax.ShapeDtypeStruct((count, channels, LAGS), BF16),
        in_specs=[vmem, vmem, vmem, smem],
        out_specs=hbm,
        scratch_shapes=[
            pltpu.VMEM((2 * group * channels, NFFT), BF16),
            pltpu.VMEM((count, channels, LAGS), BF16),
            dma((count,)),
        ],
        compiler_params=pltpu.CompilerParams(vmem_limit_bytes=24 << 20),
        name="correlate",
    )(receivers, sources, lag_table(), source_index)


def solution(mesh):
    in_specs = (P("blk", "src"), P(), P("blk"), P("blk", None))
    out_specs = P("src", "blk", None)
    return jax.shard_map(local, mesh=mesh, in_specs=in_specs, out_specs=out_specs, check_vma=False)
```

```python
import functools
import math

import jax
import jax.numpy as jnp
import ml_dtypes
import numpy as np
from jax import lax
from jax.experimental import pallas as pl
from jax.experimental.pallas import tpu as pltpu
from jax.sharding import PartitionSpec as P

S = 512
NFFT = 1024
BINS = NFFT // 2
LAGS = 512
TAPS = 64
DEC = 20
HALF = 64
LANES = 128
EDGE = 8
MESH = pl.DeviceIdType.MESH
F32 = jnp.float32
BF16 = jnp.bfloat16


def split_np(table):
    high = table.astype(np.float32).astype(ml_dtypes.bfloat16)
    low = (table - high.astype(np.float64)).astype(ml_dtypes.bfloat16)
    return high, low


def forward_tables():
    phases = 2.0 * math.pi / NFFT * (np.outer(np.arange(S), np.arange(BINS)) % NFFT)
    return split_np(np.concatenate([np.cos(phases), -np.sin(phases)], axis=1))


def band_table():
    bins = np.arange(BINS)
    return (np.abs(bins[:, None] - bins[None, :]) <= HALF).astype(ml_dtypes.bfloat16)


def lag_table():
    bins = np.arange(BINS)
    shift = np.arange(LAGS) - LAGS // 2
    phases = 2.0 * math.pi / NFFT * (np.outer(bins, shift) % NFFT)
    weight = np.where(bins[:, None] == 0, 0.5, 1.0) / math.sqrt(BINS)
    table = np.concatenate([weight * np.cos(phases), -weight * np.sin(phases)], axis=0)
    return table.astype(np.float32).astype(ml_dtypes.bfloat16)


def split(value):
    high = value.astype(BF16)
    return high, (value - high.astype(F32)).astype(BF16)


def dot(a, b):
    return jnp.dot(a, b, preferred_element_type=F32)


def dot_nt(a, b):
    return lax.dot_general(a, b, (((1,), (1,)), ((), ())), preferred_element_type=F32)


def whitened(series, high_table, low_table, band):
    rows = series.shape[0]
    high, low = split(series)
    both = dot(jnp.concatenate([high, low], axis=0), high_table)
    spectrum = both[:rows] + both[rows:] + dot(high, low_table)
    real_part, imag_part = spectrum[:, :BINS], spectrum[:, BINS:]
    high, low = split(real_part * real_part + imag_part * imag_part)
    sums = dot(jnp.concatenate([high, low], axis=0), band)
    bins = lax.broadcasted_iota(jnp.int32, (1, BINS), 1)
    count = jnp.minimum(bins, HALF) + jnp.minimum(BINS - 1 - bins, HALF) + 1
    smooth = (sums[:rows] + sums[rows:]) / count.astype(F32)
    factor = lax.rsqrt(smooth + 1e-6)
    return real_part * factor, imag_part * factor


def tap_matrix(taps, raw_count, rows, edge_row):
    row = lax.broadcasted_iota(jnp.int32, (rows, LANES), 0)
    start = DEC * jnp.where(row < edge_row, row, row - rows)
    lane = lax.broadcasted_iota(jnp.int32, (rows, LANES), 1)
    padded = jnp.concatenate([taps, jnp.zeros((1, LANES - TAPS), F32)], axis=1)
    spread = jnp.broadcast_to(padded, (rows, LANES))
    turned = jnp.take_along_axis(spread, (lane - start) & (LANES - 1), axis=1)
    high, low = split(turned)
    high, low = high.astype(F32), low.astype(F32)
    highs, lows = [], []
    for first in range(0, raw_count, LANES):
        offset = lane + first - start
        inside = (offset >= 0) & (offset < TAPS)
        highs.append(jnp.where(inside, high, 0.0).astype(BF16))
        lows.append(jnp.where(inside, low, 0.0).astype(BF16))
    return jnp.concatenate(highs, axis=1), jnp.concatenate(lows, axis=1)


def gather_kernel(
    shards,
    blocks,
    raw_hbm,
    taps_hbm,
    alive_hbm,
    index_hbm,
    high_hbm,
    low_hbm,
    band_hbm,
    receivers_ref,
    sources_ref,
    raw,
    taps,
    alive,
    index,
    high_table,
    low_table,
    band,
    parts,
    pieces,
    packed,
    arrived,
    local_sem,
    piece_send,
    piece_recv,
    part_send,
    part_recv,
    source_send,
    source_recv,
    go,
    ready,
):
    blk = lax.axis_index("blk")
    src = lax.axis_index("src")
    channels, raw_count = raw.shape
    out_rows = S // shards
    half = shards // 2
    chip = lax.div(src, 2)
    core = lax.rem(src, 2)
    sibling = 2 * chip + 1 - core
    group = lax.div(blk, shards)
    slot = lax.rem(blk, shards)
    leads = src == group
    late = lax.rem(lax.div(blk, 4), 8) >= 4

    def source_target(step):
        return lax.rem(lax.div(step, 4), 2) * (blocks // 2) + lax.div(step, 8) * 4 + lax.rem(step, 4)

    loads = [
        pltpu.make_async_copy(source, target, local_sem.at[k])
        for k, (source, target) in enumerate(
            [
                (taps_hbm, taps),
                (raw_hbm, raw),
                (alive_hbm, alive),
                (index_hbm, index),
                (high_hbm, high_table),
                (low_hbm, low_table),
                (band_hbm, band),
            ]
        )
    ]
    for load in loads[:4]:
        load.start()

    barrier = pltpu.get_barrier_semaphore()
    answers = late & (lax.rem(src, half) < half // 2)
    for step in range(1, shards):
        peer = lax.rem(src + step, shards)
        pl.semaphore_signal(barrier, inc=1, device_id=(blk, peer), device_id_type=MESH)
    for step in range(shards):
        @pl.when(jnp.logical_not(answers) & (jnp.logical_not(leads) | (slot != step)))
        def _():
            pl.semaphore_signal(
                barrier, inc=1, device_id=(src * shards + step, src), device_id_type=MESH
            )

    @pl.when(leads & jnp.logical_not(late))
    def _():
        @pl.loop(blocks // 2, blocks)
        def _(step):
            pl.semaphore_signal(
                barrier, inc=1, device_id=(source_target(step), group), device_id_type=MESH
            )


    loads[0].wait()
    tap_high, tap_low = tap_matrix(taps[...], raw_count, out_rows + EDGE, out_rows)
    for load in loads[1:4]:
        load.wait()
    for load in loads[4:]:
        load.start()
    raw_high, raw_low = split(raw[...])
    decimated = dot_nt(tap_high, raw_high) + dot_nt(tap_low, raw_high) + dot_nt(tap_high, raw_low)
    decimated = decimated * alive[...].astype(F32)
    parts[src] = decimated

    lane = lax.broadcasted_iota(jnp.int32, (8, channels), 1)
    row = lax.broadcasted_iota(jnp.int32, (8, channels), 0)
    chosen = jnp.where(row == 0, index[0, 0], jnp.where(row == 1, index[0, 1], -1))
    chooser = (lane == chosen).astype(F32).astype(BF16)
    padded = jnp.concatenate(
        [
            decimated[:out_rows],
            jnp.zeros((LANES - out_rows - EDGE, channels), F32),
            decimated[out_rows:],
        ],
        axis=0,
    )
    first, rest = split(padded)
    second, third = split(padded - first.astype(F32))
    pieces[src] = dot_nt(chooser, first) + dot_nt(chooser, second) + dot_nt(chooser, third)

    def piece_copy(shard):
        return pltpu.make_async_remote_copy(
            src_ref=pieces.at[shard],
            dst_ref=pieces.at[shard],
            send_sem=piece_send,
            recv_sem=piece_recv.at[shard],
            device_id=(blk, group),
            device_id_type=MESH,
        )

    def part_copy(shard, sem, peer):
        return pltpu.make_async_remote_copy(
            src_ref=parts.at[shard],
            dst_ref=parts.at[shard],
            send_sem=part_send.at[sem],
            recv_sem=part_recv.at[shard],
            device_id=(blk, peer),
            device_id_type=MESH,
        )

    def own_part(step):
        other = lax.rem(chip + step, half)
        heard = jnp.where(other == lax.div(group, 2), 1 - lax.rem(group, 2), core)
        return part_copy(src, step, sibling if step == 0 else 2 * other + heard)

    def handed_part(step):
        of_core = step % 2
        shard = 2 * lax.rem(chip + 1 + step // 2, half) + of_core
        hands = jnp.logical_not(leads) & ((of_core == core) | (sibling == group))
        return shard, hands, part_copy(shard, half + step, sibling)

    def await_part(shard):
        pltpu.make_async_copy(parts.at[shard], parts.at[shard], part_recv.at[shard]).wait()

    def source_copy(step):
        target = source_target(step)
        return target, pltpu.make_async_remote_copy(
            src_ref=packed,
            dst_ref=arrived.at[slot],
            send_sem=source_send.at[step],
            recv_sem=source_recv.at[slot],
            device_id=(target, group),
            device_id_type=MESH,
        )

    def send_sources(start, stop):
        @pl.loop(start, stop)
        def _(step):
            target, copy = source_copy(step)

            @pl.when(target != blk)
            def _():
                copy.start()

    @pl.when(answers)
    def _():
        pl.semaphore_wait(barrier, shards - 1 + shards)

    @pl.when(jnp.logical_not(leads | answers))
    def _():
        pl.semaphore_wait(barrier, shards - 1)

    @pl.when(leads & late)
    def _():
        pl.semaphore_wait(barrier, shards - 1 + blocks - 1)

    @pl.when(leads & jnp.logical_not(late))
    def _():
        pl.semaphore_wait(barrier, shards - 1 + blocks // 2 - 1)

    @pl.when(jnp.logical_not(leads))
    def _():
        piece_copy(src).start()

    @pl.when(answers)
    def _():
        for step in range(shards):
            pl.semaphore_signal(
                ready, inc=1, device_id=(src * shards + step, src), device_id_type=MESH
            )

    def send_parts():
        for step in range(half):
            own_part(step).start()

    @pl.when(jnp.logical_not(late))
    def _():
        send_parts()

    @pl.when(leads)
    def _():
        for step in range(1, shards):
            shard = lax.rem(src + step, shards)
            pltpu.make_async_copy(pieces.at[shard], pieces.at[shard], piece_recv.at[shard]).wait()
        lane = lax.broadcasted_iota(jnp.int32, (8, LANES), 1)
        for pair in range(half):
            after = pieces[2 * pair + 2] if 2 * pair + 2 < shards else jnp.zeros((8, LANES), F32)
            joined = pltpu.roll(pieces[2 * pair + 1], LANES // 2, 1) + jnp.where(
                lane < LANES // 2, pieces[2 * pair], after
            )
            packed[pair : pair + 1, :] = joined[0:1]
            packed[half + pair : half + pair + 1, :] = joined[1:2]

        send_sources(0, blocks // 2)

        @pl.when(late)
        def _():
            for step in range(1, shards):
                peer = lax.rem(src + step, shards)
                pl.semaphore_signal(go, inc=1, device_id=(blk, peer), device_id_type=MESH)

            send_sources(blocks // 2, blocks)

        arrived[slot] = packed[...]

    @pl.when(late)
    def _():
        @pl.when(jnp.logical_not(leads))
        def _():
            pl.semaphore_wait(go, 1)

        send_parts()

    for step in range(shards - 2):
        shard, hands, copy = handed_part(step)

        @pl.when(hands)
        def _():
            await_part(shard)
            copy.start()

    for load in loads[4:]:
        load.wait()
    await_part(sibling)
    for step in range(shards - 2):
        shard, hands, copy = handed_part(step)

        @pl.when(jnp.logical_not(hands))
        def _():
            await_part(shard)

    rows = []
    for shard in range(shards):
        rows.append(parts[shard, : out_rows - EDGE])
        tail = parts[shard, out_rows - EDGE : out_rows]
        if shard + 1 < shards:
            tail = tail + parts[shard + 1, out_rows:]
        rows.append(tail)
    series = jnp.concatenate(rows, axis=0).T
    real_part, imag_part = whitened(series, high_table[...], low_table[...], band[...])
    receivers_ref[:, :BINS] = real_part
    receivers_ref[:, BINS:] = imag_part

    @pl.when(leads & jnp.logical_not(late))
    def _():
        pl.semaphore_wait(ready, blocks // 2)
        send_sources(blocks // 2, blocks)

    for step in range(shards):
        @pl.when(jnp.logical_not(leads) | (slot != step))
        def _():
            pltpu.make_async_copy(arrived.at[step], arrived.at[step], source_recv.at[step]).wait()
    sources = jnp.concatenate(
        [
            jnp.concatenate([arrived[:, v * half + pair, :] for pair in range(half)], axis=1)
            for v in range(2)
        ],
        axis=0,
    )
    real_part, imag_part = whitened(sources, high_table[...], low_table[...], band[...])
    sources_ref[:, :BINS] = real_part
    sources_ref[:, BINS:] = imag_part

    for step in range(half):
        own_part(step).wait_send()
    for step in range(shards - 2):
        shard, hands, copy = handed_part(step)

        @pl.when(hands)
        def _():
            copy.wait_send()


    @pl.when(jnp.logical_not(leads))
    def _():
        piece_copy(src).wait_send()

    @pl.when(leads)
    def _():
        @pl.loop(0, blocks)
        def _(step):
            target, copy = source_copy(step)

            @pl.when(target != blk)
            def _():
                copy.wait_send()


def correlate_kernel(shards, group, receivers, sources, lags, index_ref, out, cross, lagged, sem):
    blk = lax.axis_index("blk")
    src = lax.axis_index("src")
    channels = receivers.shape[0]
    count = sources.shape[0]
    mine = lax.div(blk, shards) == src
    slot = lax.rem(blk, shards)

    def out_copy(row):
        local = lax.rem(row, shards) * 2 + lax.div(row, shards)
        return pltpu.make_async_copy(lagged.at[row], out.at[local], sem.at[row])

    def form(step):
        for k in range(group):
            row = step * group + k
            rows = pl.ds((step % 2 * group + k) * channels, channels)
            src_re, src_im = sources[row : row + 1, :BINS], sources[row : row + 1, BINS:]
            rec_re, rec_im = receivers[:, :BINS], receivers[:, BINS:]
            cross[rows, :BINS] = (src_re * rec_re + src_im * rec_im).astype(BF16)
            cross[rows, BINS:] = (src_re * rec_im - src_im * rec_re).astype(BF16)

    channel = lax.broadcasted_iota(jnp.int32, (channels, 1), 0)
    form(0)
    for step in range(count // group):
        if step + 1 < count // group:
            form(step + 1)
        size = group * channels
        product = dot(cross[pl.ds(step % 2 * size, size)], lags[...])
        for k in range(group):
            row = step * group + k
            chosen = jnp.where(mine & (row % shards == slot), index_ref[0, row // shards], -1)
            kept = jnp.where(channel == chosen, 0.0, product[k * channels : (k + 1) * channels])
            lagged[row] = kept.astype(BF16)
            out_copy(row).start()

    @pl.loop(0, count)
    def _(row):
        out_copy(row).wait()


def local(raw_records, fir_taps, alive_mask, source_index):
    shards = lax.axis_size("src")
    blocks = lax.axis_size("blk")
    channels, raw_count = raw_records.shape
    count = 2 * shards
    high_table, low_table = forward_tables()
    vmem = pl.BlockSpec(memory_space=pltpu.VMEM)
    smem = pl.BlockSpec(memory_space=pltpu.SMEM)
    hbm = pl.BlockSpec(memory_space=pltpu.HBM)
    dma = pltpu.SemaphoreType.DMA
    receivers, sources = pl.pallas_call(
        functools.partial(gather_kernel, shards, blocks),
        out_shape=(
            jax.ShapeDtypeStruct((channels, NFFT), F32),
            jax.ShapeDtypeStruct((count, NFFT), F32),
        ),
        in_specs=[hbm] * 7,
        out_specs=(vmem, vmem),
        scratch_shapes=[
            pltpu.VMEM((channels, raw_count), F32),
            pltpu.VMEM((1, TAPS), F32),
            pltpu.VMEM((1, channels), jnp.int32),
            pltpu.SMEM((1, 2), jnp.int32),
            pltpu.VMEM((S, NFFT), BF16),
            pltpu.VMEM((S, NFFT), BF16),
            pltpu.VMEM((BINS, BINS), BF16),
            pltpu.VMEM((shards, S // shards + EDGE, channels), F32),
            pltpu.VMEM((shards, 8, LANES), F32),
            pltpu.VMEM((8, LANES), F32),
            pltpu.VMEM((shards, 8, LANES), F32),
            dma((7,)),
            dma,
            dma((shards,)),
            dma((shards // 2 + shards - 2,)),
            dma((shards,)),
            dma((blocks,)),
            dma((shards,)),
            pltpu.SemaphoreType.REGULAR,
            pltpu.SemaphoreType.REGULAR,
        ],
        compiler_params=pltpu.CompilerParams(
            collective_id=0, has_side_effects=True, vmem_limit_bytes=24 << 20
        ),
        name="gather_whiten",
    )(
        *(
            pltpu.with_memory_space_constraint(jnp.asarray(operand), pltpu.HBM)
            for operand in (
                raw_records,
                fir_taps.reshape(1, TAPS),
                alive_mask.reshape(1, channels),
                source_index,
                high_table,
                low_table,
                band_table(),
            )
        )
    )
    group = 2
    return pl.pallas_call(
        functools.partial(correlate_kernel, shards, group),
        out_shape=jax.ShapeDtypeStruct((count, channels, LAGS), BF16),
        in_specs=[vmem, vmem, vmem, smem],
        out_specs=hbm,
        scratch_shapes=[
            pltpu.VMEM((2 * group * channels, NFFT), BF16),
            pltpu.VMEM((count, channels, LAGS), BF16),
            dma((count,)),
        ],
        compiler_params=pltpu.CompilerParams(vmem_limit_bytes=24 << 20),
        name="correlate",
    )(receivers, sources, lag_table(), source_index)


def solution(mesh):
    in_specs = (P("blk", "src"), P(), P("blk"), P("blk", None))
    out_specs = P("src", "blk", None)
    return jax.shard_map(local, mesh=mesh, in_specs=in_specs, out_specs=out_specs, check_vma=False)
```

```python
import functools
import math

import jax
import jax.numpy as jnp
import ml_dtypes
import numpy as np
from jax import lax
from jax.experimental import pallas as pl
from jax.experimental.pallas import tpu as pltpu
from jax.sharding import PartitionSpec as P

S = 512
NFFT = 1024
BINS = NFFT // 2
LAGS = 512
TAPS = 64
DEC = 20
HALF = 64
LANES = 128
EDGE = 8
MESH = pl.DeviceIdType.MESH
F32 = jnp.float32
BF16 = jnp.bfloat16


def split_np(table):
    high = table.astype(np.float32).astype(ml_dtypes.bfloat16)
    low = (table - high.astype(np.float64)).astype(ml_dtypes.bfloat16)
    return high, low


def forward_tables():
    phases = 2.0 * math.pi / NFFT * (np.outer(np.arange(S), np.arange(BINS)) % NFFT)
    return split_np(np.concatenate([np.cos(phases), -np.sin(phases)], axis=1))


def band_table():
    bins = np.arange(BINS)
    return (np.abs(bins[:, None] - bins[None, :]) <= HALF).astype(ml_dtypes.bfloat16)


def lag_table():
    bins = np.arange(BINS)
    shift = np.arange(LAGS) - LAGS // 2
    phases = 2.0 * math.pi / NFFT * (np.outer(bins, shift) % NFFT)
    weight = np.where(bins[:, None] == 0, 0.5, 1.0) / math.sqrt(BINS)
    table = np.concatenate([weight * np.cos(phases), -weight * np.sin(phases)], axis=0)
    return table.astype(np.float32).astype(ml_dtypes.bfloat16)


def split(value):
    high = value.astype(BF16)
    return high, (value - high.astype(F32)).astype(BF16)


def dot(a, b):
    return jnp.dot(a, b, preferred_element_type=F32)


def dot_nt(a, b):
    return lax.dot_general(a, b, (((1,), (1,)), ((), ())), preferred_element_type=F32)


def whitened(series, high_table, low_table, band):
    rows = series.shape[0]
    high, low = split(series)
    both = dot(jnp.concatenate([high, low], axis=0), high_table)
    spectrum = both[:rows] + both[rows:] + dot(high, low_table)
    real_part, imag_part = spectrum[:, :BINS], spectrum[:, BINS:]
    high, low = split(real_part * real_part + imag_part * imag_part)
    sums = dot(jnp.concatenate([high, low], axis=0), band)
    bins = lax.broadcasted_iota(jnp.int32, (1, BINS), 1)
    count = jnp.minimum(bins, HALF) + jnp.minimum(BINS - 1 - bins, HALF) + 1
    smooth = (sums[:rows] + sums[rows:]) / count.astype(F32)
    factor = lax.rsqrt(smooth + 1e-6)
    return real_part * factor, imag_part * factor


def tap_matrix(taps, raw_count, rows, edge_row):
    row = lax.broadcasted_iota(jnp.int32, (rows, LANES), 0)
    start = DEC * jnp.where(row < edge_row, row, row - rows)
    lane = lax.broadcasted_iota(jnp.int32, (rows, LANES), 1)
    padded = jnp.concatenate([taps, jnp.zeros((1, LANES - TAPS), F32)], axis=1)
    spread = jnp.broadcast_to(padded, (rows, LANES))
    turned = jnp.take_along_axis(spread, (lane - start) & (LANES - 1), axis=1)
    high, low = split(turned)
    high, low = high.astype(F32), low.astype(F32)
    highs, lows = [], []
    for first in range(0, raw_count, LANES):
        offset = lane + first - start
        inside = (offset >= 0) & (offset < TAPS)
        highs.append(jnp.where(inside, high, 0.0).astype(BF16))
        lows.append(jnp.where(inside, low, 0.0).astype(BF16))
    return jnp.concatenate(highs, axis=1), jnp.concatenate(lows, axis=1)


def leader_of(group):
    pair = lax.div(group, 2)
    return 2 * jnp.where(pair == 1, 3, jnp.where(pair == 3, 1, 0)) + lax.rem(group, 2)


def gather_kernel(
    shards,
    blocks,
    raw_hbm,
    taps_hbm,
    alive_hbm,
    index_hbm,
    high_hbm,
    low_hbm,
    band_hbm,
    receivers_ref,
    sources_ref,
    raw,
    taps,
    alive,
    index,
    high_table,
    low_table,
    band,
    parts,
    pieces,
    packed,
    arrived,
    local_sem,
    piece_send,
    piece_recv,
    part_send,
    part_recv,
    source_send,
    source_recv,
    go,
    ready,
):
    blk = lax.axis_index("blk")
    src = lax.axis_index("src")
    channels, raw_count = raw.shape
    out_rows = S // shards
    half = shards // 2
    chip = lax.div(src, 2)
    core = lax.rem(src, 2)
    sibling = 2 * chip + 1 - core
    group = lax.div(blk, shards)
    slot = lax.rem(blk, shards)
    head = leader_of(group)
    leads = src == head
    serves_itself = leads & (src == group)
    late = lax.rem(lax.div(blk, 4), 8) >= 4

    def source_target(step):
        return lax.rem(lax.div(step, 4), 2) * (blocks // 2) + lax.div(step, 8) * 4 + lax.rem(step, 4)

    loads = [
        pltpu.make_async_copy(source, target, local_sem.at[k])
        for k, (source, target) in enumerate(
            [
                (taps_hbm, taps),
                (raw_hbm, raw),
                (alive_hbm, alive),
                (index_hbm, index),
                (high_hbm, high_table),
                (low_hbm, low_table),
                (band_hbm, band),
            ]
        )
    ]
    for load in loads[:4]:
        load.start()

    barrier = pltpu.get_barrier_semaphore()
    answers = late & (lax.rem(src, half) < half // 2)
    for step in range(1, shards):
        peer = lax.rem(src + step, shards)
        pl.semaphore_signal(barrier, inc=1, device_id=(blk, peer), device_id_type=MESH)
    for step in range(shards):
        @pl.when(jnp.logical_not(answers | (serves_itself & (slot == step))))
        def _():
            pl.semaphore_signal(
                barrier,
                inc=1,
                device_id=(src * shards + step, leader_of(src)),
                device_id_type=MESH,
            )

    @pl.when(leads & jnp.logical_not(late))
    def _():
        @pl.loop(blocks // 2, blocks)
        def _(step):
            pl.semaphore_signal(
                barrier, inc=1, device_id=(source_target(step), group), device_id_type=MESH
            )


    loads[0].wait()
    tap_high, tap_low = tap_matrix(taps[...], raw_count, out_rows + EDGE, out_rows)
    for load in loads[1:4]:
        load.wait()
    for load in loads[4:]:
        load.start()
    raw_high, raw_low = split(raw[...])
    decimated = dot_nt(tap_high, raw_high) + dot_nt(tap_low, raw_high) + dot_nt(tap_high, raw_low)
    decimated = decimated * alive[...].astype(F32)
    parts[src] = decimated

    lane = lax.broadcasted_iota(jnp.int32, (8, channels), 1)
    row = lax.broadcasted_iota(jnp.int32, (8, channels), 0)
    chosen = jnp.where(row == 0, index[0, 0], jnp.where(row == 1, index[0, 1], -1))
    chooser = (lane == chosen).astype(F32).astype(BF16)
    padded = jnp.concatenate(
        [
            decimated[:out_rows],
            jnp.zeros((LANES - out_rows - EDGE, channels), F32),
            decimated[out_rows:],
        ],
        axis=0,
    )
    first, rest = split(padded)
    second, third = split(padded - first.astype(F32))
    pieces[src] = dot_nt(chooser, first) + dot_nt(chooser, second) + dot_nt(chooser, third)

    def piece_copy(shard):
        return pltpu.make_async_remote_copy(
            src_ref=pieces.at[shard],
            dst_ref=pieces.at[shard],
            send_sem=piece_send,
            recv_sem=piece_recv.at[shard],
            device_id=(blk, head),
            device_id_type=MESH,
        )

    def part_copy(shard, sem, peer):
        return pltpu.make_async_remote_copy(
            src_ref=parts.at[shard],
            dst_ref=parts.at[shard],
            send_sem=part_send.at[sem],
            recv_sem=part_recv.at[shard],
            device_id=(blk, peer),
            device_id_type=MESH,
        )

    def own_part(step):
        other = lax.rem(chip + step, half)
        heard = jnp.where(other == lax.div(head, 2), 1 - lax.rem(head, 2), core)
        return part_copy(src, step, sibling if step == 0 else 2 * other + heard)

    def handed_part(step):
        of_core = step % 2
        shard = 2 * lax.rem(chip + 1 + step // 2, half) + of_core
        hands = jnp.logical_not(leads) & ((of_core == core) | (sibling == head))
        return shard, hands, part_copy(shard, half + step, sibling)

    def await_part(shard):
        pltpu.make_async_copy(parts.at[shard], parts.at[shard], part_recv.at[shard]).wait()

    def source_copy(step):
        target = source_target(step)
        return target, pltpu.make_async_remote_copy(
            src_ref=packed,
            dst_ref=arrived.at[slot],
            send_sem=source_send.at[step],
            recv_sem=source_recv.at[slot],
            device_id=(target, group),
            device_id_type=MESH,
        )

    def send_sources(start, stop):
        @pl.loop(start, stop)
        def _(step):
            target, copy = source_copy(step)

            @pl.when((target != blk) | (src != group))
            def _():
                copy.start()

    @pl.when(answers)
    def _():
        pl.semaphore_wait(barrier, shards - 1 + shards)

    @pl.when(jnp.logical_not(leads | answers))
    def _():
        pl.semaphore_wait(barrier, shards - 1)

    for served, count in ((late, blocks), (jnp.logical_not(late), blocks // 2)):
        @pl.when(leads & served & (src == group))
        def _():
            pl.semaphore_wait(barrier, shards - 1 + count - 1)

        @pl.when(leads & served & (src != group))
        def _():
            pl.semaphore_wait(barrier, shards - 1 + count)

    @pl.when(jnp.logical_not(leads))
    def _():
        piece_copy(src).start()

    @pl.when(answers)
    def _():
        for step in range(shards):
            pl.semaphore_signal(
                ready,
                inc=1,
                device_id=(src * shards + step, leader_of(src)),
                device_id_type=MESH,
            )

    def send_parts():
        for step in range(half):
            own_part(step).start()

    @pl.when(jnp.logical_not(late))
    def _():
        send_parts()

    @pl.when(leads)
    def _():
        for step in range(1, shards):
            shard = lax.rem(src + step, shards)
            pltpu.make_async_copy(pieces.at[shard], pieces.at[shard], piece_recv.at[shard]).wait()
        lane = lax.broadcasted_iota(jnp.int32, (8, LANES), 1)
        for pair in range(half):
            after = pieces[2 * pair + 2] if 2 * pair + 2 < shards else jnp.zeros((8, LANES), F32)
            joined = pltpu.roll(pieces[2 * pair + 1], LANES // 2, 1) + jnp.where(
                lane < LANES // 2, pieces[2 * pair], after
            )
            packed[pair : pair + 1, :] = joined[0:1]
            packed[half + pair : half + pair + 1, :] = joined[1:2]

        send_sources(0, blocks // 2)

        @pl.when(late)
        def _():
            for step in range(1, shards):
                peer = lax.rem(src + step, shards)
                pl.semaphore_signal(go, inc=1, device_id=(blk, peer), device_id_type=MESH)

            send_sources(blocks // 2, blocks)

        @pl.when(serves_itself)
        def _():
            arrived[slot] = packed[...]

    @pl.when(late)
    def _():
        @pl.when(jnp.logical_not(leads))
        def _():
            pl.semaphore_wait(go, 1)

        send_parts()

    for step in range(shards - 2):
        shard, hands, copy = handed_part(step)

        @pl.when(hands)
        def _():
            await_part(shard)
            copy.start()

    for load in loads[4:]:
        load.wait()
    await_part(sibling)
    for step in range(shards - 2):
        shard, hands, copy = handed_part(step)

        @pl.when(jnp.logical_not(hands))
        def _():
            await_part(shard)

    rows = []
    for shard in range(shards):
        rows.append(parts[shard, : out_rows - EDGE])
        tail = parts[shard, out_rows - EDGE : out_rows]
        if shard + 1 < shards:
            tail = tail + parts[shard + 1, out_rows:]
        rows.append(tail)
    series = jnp.concatenate(rows, axis=0).T
    real_part, imag_part = whitened(series, high_table[...], low_table[...], band[...])
    receivers_ref[:, :BINS] = real_part
    receivers_ref[:, BINS:] = imag_part

    @pl.when(leads & jnp.logical_not(late))
    def _():
        pl.semaphore_wait(ready, blocks // 2)
        send_sources(blocks // 2, blocks)

    for step in range(shards):
        @pl.when(jnp.logical_not(serves_itself & (slot == step)))
        def _():
            pltpu.make_async_copy(arrived.at[step], arrived.at[step], source_recv.at[step]).wait()
    sources = jnp.concatenate(
        [
            jnp.concatenate([arrived[:, v * half + pair, :] for pair in range(half)], axis=1)
            for v in range(2)
        ],
        axis=0,
    )
    real_part, imag_part = whitened(sources, high_table[...], low_table[...], band[...])
    sources_ref[:, :BINS] = real_part
    sources_ref[:, BINS:] = imag_part

    for step in range(half):
        own_part(step).wait_send()
    for step in range(shards - 2):
        shard, hands, copy = handed_part(step)

        @pl.when(hands)
        def _():
            copy.wait_send()


    @pl.when(jnp.logical_not(leads))
    def _():
        piece_copy(src).wait_send()

    @pl.when(leads)
    def _():
        @pl.loop(0, blocks)
        def _(step):
            target, copy = source_copy(step)

            @pl.when((target != blk) | (src != group))
            def _():
                copy.wait_send()


def correlate_kernel(shards, group, receivers, sources, lags, index_ref, out, cross, lagged, sem):
    blk = lax.axis_index("blk")
    src = lax.axis_index("src")
    channels = receivers.shape[0]
    count = sources.shape[0]
    mine = lax.div(blk, shards) == src
    slot = lax.rem(blk, shards)

    def out_copy(row):
        local = lax.rem(row, shards) * 2 + lax.div(row, shards)
        return pltpu.make_async_copy(lagged.at[row], out.at[local], sem.at[row])

    def form(step):
        for k in range(group):
            row = step * group + k
            rows = pl.ds((step % 2 * group + k) * channels, channels)
            src_re, src_im = sources[row : row + 1, :BINS], sources[row : row + 1, BINS:]
            rec_re, rec_im = receivers[:, :BINS], receivers[:, BINS:]
            cross[rows, :BINS] = (src_re * rec_re + src_im * rec_im).astype(BF16)
            cross[rows, BINS:] = (src_re * rec_im - src_im * rec_re).astype(BF16)

    channel = lax.broadcasted_iota(jnp.int32, (channels, 1), 0)
    form(0)
    for step in range(count // group):
        if step + 1 < count // group:
            form(step + 1)
        size = group * channels
        product = dot(cross[pl.ds(step % 2 * size, size)], lags[...])
        for k in range(group):
            row = step * group + k
            chosen = jnp.where(mine & (row % shards == slot), index_ref[0, row // shards], -1)
            kept = jnp.where(channel == chosen, 0.0, product[k * channels : (k + 1) * channels])
            lagged[row] = kept.astype(BF16)
            out_copy(row).start()

    @pl.loop(0, count)
    def _(row):
        out_copy(row).wait()


def local(raw_records, fir_taps, alive_mask, source_index):
    shards = lax.axis_size("src")
    blocks = lax.axis_size("blk")
    channels, raw_count = raw_records.shape
    count = 2 * shards
    high_table, low_table = forward_tables()
    vmem = pl.BlockSpec(memory_space=pltpu.VMEM)
    smem = pl.BlockSpec(memory_space=pltpu.SMEM)
    hbm = pl.BlockSpec(memory_space=pltpu.HBM)
    dma = pltpu.SemaphoreType.DMA
    receivers, sources = pl.pallas_call(
        functools.partial(gather_kernel, shards, blocks),
        out_shape=(
            jax.ShapeDtypeStruct((channels, NFFT), F32),
            jax.ShapeDtypeStruct((count, NFFT), F32),
        ),
        in_specs=[hbm] * 7,
        out_specs=(vmem, vmem),
        scratch_shapes=[
            pltpu.VMEM((channels, raw_count), F32),
            pltpu.VMEM((1, TAPS), F32),
            pltpu.VMEM((1, channels), jnp.int32),
            pltpu.SMEM((1, 2), jnp.int32),
            pltpu.VMEM((S, NFFT), BF16),
            pltpu.VMEM((S, NFFT), BF16),
            pltpu.VMEM((BINS, BINS), BF16),
            pltpu.VMEM((shards, S // shards + EDGE, channels), F32),
            pltpu.VMEM((shards, 8, LANES), F32),
            pltpu.VMEM((8, LANES), F32),
            pltpu.VMEM((shards, 8, LANES), F32),
            dma((7,)),
            dma,
            dma((shards,)),
            dma((shards // 2 + shards - 2,)),
            dma((shards,)),
            dma((blocks,)),
            dma((shards,)),
            pltpu.SemaphoreType.REGULAR,
            pltpu.SemaphoreType.REGULAR,
        ],
        compiler_params=pltpu.CompilerParams(
            collective_id=0, has_side_effects=True, vmem_limit_bytes=24 << 20
        ),
        name="gather_whiten",
    )(
        *(
            pltpu.with_memory_space_constraint(jnp.asarray(operand), pltpu.HBM)
            for operand in (
                raw_records,
                fir_taps.reshape(1, TAPS),
                alive_mask.reshape(1, channels),
                source_index,
                high_table,
                low_table,
                band_table(),
            )
        )
    )
    group = 2
    return pl.pallas_call(
        functools.partial(correlate_kernel, shards, group),
        out_shape=jax.ShapeDtypeStruct((count, channels, LAGS), BF16),
        in_specs=[vmem, vmem, vmem, smem],
        out_specs=hbm,
        scratch_shapes=[
            pltpu.VMEM((2 * group * channels, NFFT), BF16),
            pltpu.VMEM((count, channels, LAGS), BF16),
            dma((count,)),
        ],
        compiler_params=pltpu.CompilerParams(vmem_limit_bytes=24 << 20),
        name="correlate",
    )(receivers, sources, lag_table(), source_index)


def solution(mesh):
    in_specs = (P("blk", "src"), P(), P("blk"), P("blk", None))
    out_specs = P("src", "blk", None)
    return jax.shard_map(local, mesh=mesh, in_specs=in_specs, out_specs=out_specs, check_vma=False)
```

```python
import functools
import math

import jax
import jax.numpy as jnp
import ml_dtypes
import numpy as np
from jax import lax
from jax.experimental import pallas as pl
from jax.experimental.pallas import tpu as pltpu
from jax.sharding import PartitionSpec as P

S = 512
NFFT = 1024
BINS = NFFT // 2
LAGS = 512
TAPS = 64
DEC = 20
HALF = 64
LANES = 128
EDGE = 8
MESH = pl.DeviceIdType.MESH
F32 = jnp.float32
BF16 = jnp.bfloat16


def split_np(table):
    high = table.astype(np.float32).astype(ml_dtypes.bfloat16)
    low = (table - high.astype(np.float64)).astype(ml_dtypes.bfloat16)
    return high, low


def forward_tables():
    phases = 2.0 * math.pi / NFFT * (np.outer(np.arange(S), np.arange(BINS)) % NFFT)
    return split_np(np.concatenate([np.cos(phases), -np.sin(phases)], axis=1))


def band_table():
    bins = np.arange(BINS)
    return (np.abs(bins[:, None] - bins[None, :]) <= HALF).astype(ml_dtypes.bfloat16)


def lag_table():
    bins = np.arange(BINS)
    shift = np.arange(LAGS) - LAGS // 2
    phases = 2.0 * math.pi / NFFT * (np.outer(bins, shift) % NFFT)
    weight = np.where(bins[:, None] == 0, 0.5, 1.0) / math.sqrt(BINS)
    table = np.concatenate([weight * np.cos(phases), -weight * np.sin(phases)], axis=0)
    return table.astype(np.float32).astype(ml_dtypes.bfloat16)


def split(value):
    high = value.astype(BF16)
    return high, (value - high.astype(F32)).astype(BF16)


def dot(a, b):
    return jnp.dot(a, b, preferred_element_type=F32)


def dot_nt(a, b):
    return lax.dot_general(a, b, (((1,), (1,)), ((), ())), preferred_element_type=F32)


def whitened(series, high_table, low_table, band):
    rows = series.shape[0]
    high, low = split(series)
    both = dot(jnp.concatenate([high, low], axis=0), high_table)
    spectrum = both[:rows] + both[rows:] + dot(high, low_table)
    real_part, imag_part = spectrum[:, :BINS], spectrum[:, BINS:]
    high, low = split(real_part * real_part + imag_part * imag_part)
    sums = dot(jnp.concatenate([high, low], axis=0), band)
    bins = lax.broadcasted_iota(jnp.int32, (1, BINS), 1)
    count = jnp.minimum(bins, HALF) + jnp.minimum(BINS - 1 - bins, HALF) + 1
    smooth = (sums[:rows] + sums[rows:]) / count.astype(F32)
    factor = lax.rsqrt(smooth + 1e-6)
    return real_part * factor, imag_part * factor


def tap_matrix(taps, raw_count, rows, edge_row):
    row = lax.broadcasted_iota(jnp.int32, (rows, LANES), 0)
    start = DEC * jnp.where(row < edge_row, row, row - rows)
    lane = lax.broadcasted_iota(jnp.int32, (rows, LANES), 1)
    padded = jnp.concatenate([taps, jnp.zeros((1, LANES - TAPS), F32)], axis=1)
    spread = jnp.broadcast_to(padded, (rows, LANES))
    turned = jnp.take_along_axis(spread, (lane - start) & (LANES - 1), axis=1)
    high, low = split(turned)
    high, low = high.astype(F32), low.astype(F32)
    highs, lows = [], []
    for first in range(0, raw_count, LANES):
        offset = lane + first - start
        inside = (offset >= 0) & (offset < TAPS)
        highs.append(jnp.where(inside, high, 0.0).astype(BF16))
        lows.append(jnp.where(inside, low, 0.0).astype(BF16))
    return jnp.concatenate(highs, axis=1), jnp.concatenate(lows, axis=1)


def leader_of(group):
    pair = lax.div(group, 2)
    return 2 * jnp.where(pair == 1, 2, jnp.where(pair == 3, 1, 0)) + lax.rem(group, 2)


def gather_kernel(
    shards,
    blocks,
    raw_hbm,
    taps_hbm,
    alive_hbm,
    index_hbm,
    high_hbm,
    low_hbm,
    band_hbm,
    receivers_ref,
    sources_ref,
    raw,
    taps,
    alive,
    index,
    high_table,
    low_table,
    band,
    parts,
    pieces,
    packed,
    arrived,
    local_sem,
    piece_send,
    piece_recv,
    part_send,
    part_recv,
    source_send,
    source_recv,
    go,
    ready,
):
    blk = lax.axis_index("blk")
    src = lax.axis_index("src")
    channels, raw_count = raw.shape
    out_rows = S // shards
    half = shards // 2
    chip = lax.div(src, 2)
    core = lax.rem(src, 2)
    sibling = 2 * chip + 1 - core
    group = lax.div(blk, shards)
    slot = lax.rem(blk, shards)
    head = leader_of(group)
    leads = src == head
    serves_itself = leads & (src == group)
    late = lax.rem(lax.div(blk, 4), 8) >= 4

    def source_target(step):
        return lax.rem(lax.div(step, 4), 2) * (blocks // 2) + lax.div(step, 8) * 4 + lax.rem(step, 4)

    loads = [
        pltpu.make_async_copy(source, target, local_sem.at[k])
        for k, (source, target) in enumerate(
            [
                (taps_hbm, taps),
                (raw_hbm, raw),
                (alive_hbm, alive),
                (index_hbm, index),
                (high_hbm, high_table),
                (low_hbm, low_table),
                (band_hbm, band),
            ]
        )
    ]
    for load in loads[:4]:
        load.start()

    barrier = pltpu.get_barrier_semaphore()
    answers = late & (
        (lax.rem(src, half) < half // 2) | ((lax.div(src, 2) == 1) & (blk >= blocks // 2))
    )
    defers_late = leads & jnp.logical_not(late)
    defers_upper = leads & (lax.div(group, 2) == 1)
    deferred = jnp.where(defers_late, blocks // 2, jnp.where(defers_upper, blocks // 4, 0))
    greeted = jnp.where(late & jnp.logical_not(leads), 1, shards - 1)
    awaited = (
        greeted
        + jnp.where(leads, blocks - deferred, 0)
        - jnp.where(serves_itself, 1, 0)
        + jnp.where(answers, shards, 0)
    )
    for step in range(1, shards):
        peer = lax.rem(src + step, shards)

        @pl.when(jnp.logical_not(late) | leads | (peer == head))
        def _():
            pl.semaphore_signal(barrier, inc=1, device_id=(blk, peer), device_id_type=MESH)

    for step in range(shards):
        @pl.when(jnp.logical_not(answers | (serves_itself & (slot == step))))
        def _():
            pl.semaphore_signal(
                barrier,
                inc=1,
                device_id=(src * shards + step, leader_of(src)),
                device_id_type=MESH,
            )

    def is_deferred(step):
        upper = lax.rem(lax.div(step, 4), 2) == 1
        return (step >= blocks // 2) & (defers_late | (defers_upper & upper))

    @pl.when(deferred > 0)
    def _():
        @pl.loop(blocks // 2, blocks)
        def _(step):
            @pl.when(is_deferred(step))
            def _():
                pl.semaphore_signal(
                    barrier, inc=1, device_id=(source_target(step), group), device_id_type=MESH
                )


    loads[0].wait()
    tap_high, tap_low = tap_matrix(taps[...], raw_count, out_rows + EDGE, out_rows)
    for load in loads[1:4]:
        load.wait()
    for load in loads[4:]:
        load.start()
    raw_high, raw_low = split(raw[...])
    decimated = dot_nt(tap_high, raw_high) + dot_nt(tap_low, raw_high) + dot_nt(tap_high, raw_low)
    decimated = decimated * alive[...].astype(F32)
    parts[src] = decimated

    lane = lax.broadcasted_iota(jnp.int32, (8, channels), 1)
    row = lax.broadcasted_iota(jnp.int32, (8, channels), 0)
    chosen = jnp.where(row == 0, index[0, 0], jnp.where(row == 1, index[0, 1], -1))
    chooser = (lane == chosen).astype(F32).astype(BF16)
    padded = jnp.concatenate(
        [
            decimated[:out_rows],
            jnp.zeros((LANES - out_rows - EDGE, channels), F32),
            decimated[out_rows:],
        ],
        axis=0,
    )
    first, rest = split(padded)
    second, third = split(padded - first.astype(F32))
    pieces[src] = dot_nt(chooser, first) + dot_nt(chooser, second) + dot_nt(chooser, third)

    def piece_copy(shard):
        return pltpu.make_async_remote_copy(
            src_ref=pieces.at[shard],
            dst_ref=pieces.at[shard],
            send_sem=piece_send,
            recv_sem=piece_recv.at[shard],
            device_id=(blk, head),
            device_id_type=MESH,
        )

    def part_copy(shard, sem, peer):
        return pltpu.make_async_remote_copy(
            src_ref=parts.at[shard],
            dst_ref=parts.at[shard],
            send_sem=part_send.at[sem],
            recv_sem=part_recv.at[shard],
            device_id=(blk, peer),
            device_id_type=MESH,
        )

    def own_part(step):
        other = lax.rem(chip + step, half)
        heard = jnp.where(other == lax.div(head, 2), 1 - lax.rem(head, 2), core)
        return part_copy(src, step, sibling if step == 0 else 2 * other + heard)

    def handed_part(step):
        of_core = step % 2
        shard = 2 * lax.rem(chip + 1 + step // 2, half) + of_core
        hands = jnp.logical_not(leads) & ((of_core == core) | (sibling == head))
        return shard, hands, part_copy(shard, half + step, sibling)

    def await_part(shard):
        pltpu.make_async_copy(parts.at[shard], parts.at[shard], part_recv.at[shard]).wait()

    def source_copy(step):
        target = source_target(step)
        return target, pltpu.make_async_remote_copy(
            src_ref=packed,
            dst_ref=arrived.at[slot],
            send_sem=source_send.at[step],
            recv_sem=source_recv.at[slot],
            device_id=(target, group),
            device_id_type=MESH,
        )

    def send_sources(start, stop, later):
        @pl.loop(start, stop)
        def _(step):
            target, copy = source_copy(step)
            turn = is_deferred(step) if later else jnp.logical_not(is_deferred(step))

            @pl.when(turn & ((target != blk) | (src != group)))
            def _():
                copy.start()

    def send_deferred():
        pl.semaphore_wait(ready, deferred)
        send_sources(blocks // 2, blocks, True)

    pl.semaphore_wait(barrier, awaited)

    @pl.when(jnp.logical_not(leads))
    def _():
        piece_copy(src).start()

    @pl.when(answers)
    def _():
        for step in range(shards):
            pl.semaphore_signal(
                ready,
                inc=1,
                device_id=(src * shards + step, leader_of(src)),
                device_id_type=MESH,
            )

    def send_parts():
        for step in range(half):
            own_part(step).start()

    @pl.when(jnp.logical_not(late))
    def _():
        send_parts()

    @pl.when(leads)
    def _():
        for step in range(1, shards):
            shard = lax.rem(src + step, shards)
            pltpu.make_async_copy(pieces.at[shard], pieces.at[shard], piece_recv.at[shard]).wait()
        lane = lax.broadcasted_iota(jnp.int32, (8, LANES), 1)
        for pair in range(half):
            after = pieces[2 * pair + 2] if 2 * pair + 2 < shards else jnp.zeros((8, LANES), F32)
            joined = pltpu.roll(pieces[2 * pair + 1], LANES // 2, 1) + jnp.where(
                lane < LANES // 2, pieces[2 * pair], after
            )
            packed[pair : pair + 1, :] = joined[0:1]
            packed[half + pair : half + pair + 1, :] = joined[1:2]

        send_sources(0, blocks // 2, False)

        @pl.when(late)
        def _():
            for step in range(1, shards):
                peer = lax.rem(src + step, shards)
                pl.semaphore_signal(go, inc=1, device_id=(blk, peer), device_id_type=MESH)

            send_sources(blocks // 2, blocks, False)

        @pl.when(serves_itself)
        def _():
            arrived[slot] = packed[...]

    @pl.when(late)
    def _():
        @pl.when(jnp.logical_not(leads))
        def _():
            pl.semaphore_wait(go, 1)

        send_parts()

        @pl.when(defers_upper)
        def _():
            send_deferred()

    for step in range(shards - 2):
        shard, hands, copy = handed_part(step)

        @pl.when(hands)
        def _():
            await_part(shard)
            copy.start()

    for load in loads[4:]:
        load.wait()
    await_part(sibling)
    for step in range(shards - 2):
        shard, hands, copy = handed_part(step)

        @pl.when(jnp.logical_not(hands))
        def _():
            await_part(shard)

    rows = []
    for shard in range(shards):
        rows.append(parts[shard, : out_rows - EDGE])
        tail = parts[shard, out_rows - EDGE : out_rows]
        if shard + 1 < shards:
            tail = tail + parts[shard + 1, out_rows:]
        rows.append(tail)
    series = jnp.concatenate(rows, axis=0).T
    real_part, imag_part = whitened(series, high_table[...], low_table[...], band[...])
    receivers_ref[:, :BINS] = real_part
    receivers_ref[:, BINS:] = imag_part

    @pl.when(defers_late)
    def _():
        send_deferred()

    for step in range(shards):
        @pl.when(jnp.logical_not(serves_itself & (slot == step)))
        def _():
            pltpu.make_async_copy(arrived.at[step], arrived.at[step], source_recv.at[step]).wait()
    sources = jnp.concatenate(
        [
            jnp.concatenate([arrived[:, v * half + pair, :] for pair in range(half)], axis=1)
            for v in range(2)
        ],
        axis=0,
    )
    real_part, imag_part = whitened(sources, high_table[...], low_table[...], band[...])
    sources_ref[:, :BINS] = real_part
    sources_ref[:, BINS:] = imag_part

    for step in range(half):
        own_part(step).wait_send()
    for step in range(shards - 2):
        shard, hands, copy = handed_part(step)

        @pl.when(hands)
        def _():
            copy.wait_send()


    @pl.when(jnp.logical_not(leads))
    def _():
        piece_copy(src).wait_send()

    @pl.when(leads)
    def _():
        @pl.loop(0, blocks)
        def _(step):
            target, copy = source_copy(step)

            @pl.when((target != blk) | (src != group))
            def _():
                copy.wait_send()


def correlate_kernel(shards, group, receivers, sources, lags, index_ref, out, cross, lagged, sem):
    blk = lax.axis_index("blk")
    src = lax.axis_index("src")
    channels = receivers.shape[0]
    count = sources.shape[0]
    mine = lax.div(blk, shards) == src
    slot = lax.rem(blk, shards)

    def out_copy(row):
        local = lax.rem(row, shards) * 2 + lax.div(row, shards)
        return pltpu.make_async_copy(lagged.at[row], out.at[local], sem.at[row])

    def form(step):
        for k in range(group):
            row = step * group + k
            rows = pl.ds((step % 2 * group + k) * channels, channels)
            src_re, src_im = sources[row : row + 1, :BINS], sources[row : row + 1, BINS:]
            rec_re, rec_im = receivers[:, :BINS], receivers[:, BINS:]
            cross[rows, :BINS] = (src_re * rec_re + src_im * rec_im).astype(BF16)
            cross[rows, BINS:] = (src_re * rec_im - src_im * rec_re).astype(BF16)

    channel = lax.broadcasted_iota(jnp.int32, (channels, 1), 0)
    form(0)
    for step in range(count // group):
        if step + 1 < count // group:
            form(step + 1)
        size = group * channels
        product = dot(cross[pl.ds(step % 2 * size, size)], lags[...])
        for k in range(group):
            row = step * group + k
            chosen = jnp.where(mine & (row % shards == slot), index_ref[0, row // shards], -1)
            kept = jnp.where(channel == chosen, 0.0, product[k * channels : (k + 1) * channels])
            lagged[row] = kept.astype(BF16)
            out_copy(row).start()

    @pl.loop(0, count)
    def _(row):
        out_copy(row).wait()


def local(raw_records, fir_taps, alive_mask, source_index):
    shards = lax.axis_size("src")
    blocks = lax.axis_size("blk")
    channels, raw_count = raw_records.shape
    count = 2 * shards
    high_table, low_table = forward_tables()
    vmem = pl.BlockSpec(memory_space=pltpu.VMEM)
    smem = pl.BlockSpec(memory_space=pltpu.SMEM)
    hbm = pl.BlockSpec(memory_space=pltpu.HBM)
    dma = pltpu.SemaphoreType.DMA
    receivers, sources = pl.pallas_call(
        functools.partial(gather_kernel, shards, blocks),
        out_shape=(
            jax.ShapeDtypeStruct((channels, NFFT), F32),
            jax.ShapeDtypeStruct((count, NFFT), F32),
        ),
        in_specs=[hbm] * 7,
        out_specs=(vmem, vmem),
        scratch_shapes=[
            pltpu.VMEM((channels, raw_count), F32),
            pltpu.VMEM((1, TAPS), F32),
            pltpu.VMEM((1, channels), jnp.int32),
            pltpu.SMEM((1, 2), jnp.int32),
            pltpu.VMEM((S, NFFT), BF16),
            pltpu.VMEM((S, NFFT), BF16),
            pltpu.VMEM((BINS, BINS), BF16),
            pltpu.VMEM((shards, S // shards + EDGE, channels), F32),
            pltpu.VMEM((shards, 8, LANES), F32),
            pltpu.VMEM((8, LANES), F32),
            pltpu.VMEM((shards, 8, LANES), F32),
            dma((7,)),
            dma,
            dma((shards,)),
            dma((shards // 2 + shards - 2,)),
            dma((shards,)),
            dma((blocks,)),
            dma((shards,)),
            pltpu.SemaphoreType.REGULAR,
            pltpu.SemaphoreType.REGULAR,
        ],
        compiler_params=pltpu.CompilerParams(
            collective_id=0, has_side_effects=True, vmem_limit_bytes=24 << 20
        ),
        name="gather_whiten",
    )(
        *(
            pltpu.with_memory_space_constraint(jnp.asarray(operand), pltpu.HBM)
            for operand in (
                raw_records,
                fir_taps.reshape(1, TAPS),
                alive_mask.reshape(1, channels),
                source_index,
                high_table,
                low_table,
                band_table(),
            )
        )
    )
    group = 2
    return pl.pallas_call(
        functools.partial(correlate_kernel, shards, group),
        out_shape=jax.ShapeDtypeStruct((count, channels, LAGS), BF16),
        in_specs=[vmem, vmem, vmem, smem],
        out_specs=hbm,
        scratch_shapes=[
            pltpu.VMEM((2 * group * channels, NFFT), BF16),
            pltpu.VMEM((count, channels, LAGS), BF16),
            dma((count,)),
        ],
        compiler_params=pltpu.CompilerParams(vmem_limit_bytes=24 << 20),
        name="correlate",
    )(receivers, sources, lag_table(), source_index)


def solution(mesh):
    in_specs = (P("blk", "src"), P(), P("blk"), P("blk", None))
    out_specs = P("src", "blk", None)
    return jax.shard_map(local, mesh=mesh, in_specs=in_specs, out_specs=out_specs, check_vma=False)
```

```python
import functools
import math

import jax
import jax.numpy as jnp
import ml_dtypes
import numpy as np
from jax import lax
from jax.experimental import pallas as pl
from jax.experimental.pallas import tpu as pltpu
from jax.sharding import PartitionSpec as P

S = 512
NFFT = 1024
BINS = NFFT // 2
LAGS = 512
TAPS = 64
DEC = 20
HALF = 64
LANES = 128
EDGE = 8
MESH = pl.DeviceIdType.MESH
F32 = jnp.float32
BF16 = jnp.bfloat16


def split_np(table):
    high = table.astype(np.float32).astype(ml_dtypes.bfloat16)
    low = (table - high.astype(np.float64)).astype(ml_dtypes.bfloat16)
    return high, low


def forward_tables():
    phases = 2.0 * math.pi / NFFT * (np.outer(np.arange(S), np.arange(BINS)) % NFFT)
    return split_np(np.concatenate([np.cos(phases), -np.sin(phases)], axis=1))


def band_table():
    bins = np.arange(BINS)
    return (np.abs(bins[:, None] - bins[None, :]) <= HALF).astype(ml_dtypes.bfloat16)


def lag_table():
    bins = np.arange(BINS)
    shift = np.arange(LAGS) - LAGS // 2
    phases = 2.0 * math.pi / NFFT * (np.outer(bins, shift) % NFFT)
    weight = np.where(bins[:, None] == 0, 0.5, 1.0) / math.sqrt(BINS)
    table = np.concatenate([weight * np.cos(phases), -weight * np.sin(phases)], axis=0)
    return table.astype(np.float32).astype(ml_dtypes.bfloat16)


def split(value):
    high = value.astype(BF16)
    return high, (value - high.astype(F32)).astype(BF16)


def dot(a, b):
    return jnp.dot(a, b, preferred_element_type=F32)


def dot_nt(a, b):
    return lax.dot_general(a, b, (((1,), (1,)), ((), ())), preferred_element_type=F32)


def whitened(series, high_table, low_table, band):
    rows = series.shape[0]
    high, low = split(series)
    both = dot(jnp.concatenate([high, low], axis=0), high_table)
    spectrum = both[:rows] + both[rows:] + dot(high, low_table)
    real_part, imag_part = spectrum[:, :BINS], spectrum[:, BINS:]
    high, low = split(real_part * real_part + imag_part * imag_part)
    sums = dot(jnp.concatenate([high, low], axis=0), band)
    bins = lax.broadcasted_iota(jnp.int32, (1, BINS), 1)
    count = jnp.minimum(bins, HALF) + jnp.minimum(BINS - 1 - bins, HALF) + 1
    smooth = (sums[:rows] + sums[rows:]) / count.astype(F32)
    factor = lax.rsqrt(smooth + 1e-6)
    return real_part * factor, imag_part * factor


def tap_matrix(taps, raw_count, rows, edge_row):
    row = lax.broadcasted_iota(jnp.int32, (rows, LANES), 0)
    start = DEC * jnp.where(row < edge_row, row, row - rows)
    lane = lax.broadcasted_iota(jnp.int32, (rows, LANES), 1)
    padded = jnp.concatenate([taps, jnp.zeros((1, LANES - TAPS), F32)], axis=1)
    spread = jnp.broadcast_to(padded, (rows, LANES))
    turned = jnp.take_along_axis(spread, (lane - start) & (LANES - 1), axis=1)
    high, low = split(turned)
    high, low = high.astype(F32), low.astype(F32)
    highs, lows = [], []
    for first in range(0, raw_count, LANES):
        offset = lane + first - start
        inside = (offset >= 0) & (offset < TAPS)
        highs.append(jnp.where(inside, high, 0.0).astype(BF16))
        lows.append(jnp.where(inside, low, 0.0).astype(BF16))
    return jnp.concatenate(highs, axis=1), jnp.concatenate(lows, axis=1)


def leader_of(group):
    pair = lax.div(group, 2)
    return 2 * jnp.where(pair == 1, 2, jnp.where(pair == 3, 1, 0)) + lax.rem(group, 2)


def gather_kernel(
    shards,
    blocks,
    raw_hbm,
    taps_hbm,
    alive_hbm,
    index_hbm,
    high_hbm,
    low_hbm,
    band_hbm,
    receivers_ref,
    sources_ref,
    own_ref,
    raw,
    taps,
    alive,
    index,
    high_table,
    low_table,
    band,
    parts,
    pieces,
    packed,
    arrived,
    local_sem,
    piece_send,
    piece_recv,
    part_send,
    part_recv,
    source_send,
    source_recv,
    go,
    ready,
):
    blk = lax.axis_index("blk")
    src = lax.axis_index("src")
    channels, raw_count = raw.shape
    out_rows = S // shards
    half = shards // 2
    chip = lax.div(src, 2)
    core = lax.rem(src, 2)
    sibling = 2 * chip + 1 - core
    group = lax.div(blk, shards)
    slot = lax.rem(blk, shards)
    head = leader_of(group)
    leads = src == head
    serves_itself = leads & (src == group)
    late = lax.rem(lax.div(blk, 4), 8) >= 4

    def source_target(step):
        return lax.rem(lax.div(step, 4), 2) * (blocks // 2) + lax.div(step, 8) * 4 + lax.rem(step, 4)

    loads = [
        pltpu.make_async_copy(source, target, local_sem.at[k])
        for k, (source, target) in enumerate(
            [
                (taps_hbm, taps),
                (raw_hbm, raw),
                (alive_hbm, alive),
                (index_hbm, index),
                (high_hbm, high_table),
                (low_hbm, low_table),
                (band_hbm, band),
            ]
        )
    ]
    for load in loads[:4]:
        load.start()

    barrier = pltpu.get_barrier_semaphore()
    answers = late & (
        (lax.rem(src, half) < half // 2) | ((lax.div(src, 2) == 1) & (blk >= blocks // 2))
    )
    defers_late = leads & jnp.logical_not(late)
    defers_upper = leads & (lax.div(group, 2) == 1)
    deferred = jnp.where(defers_late, blocks // 2, jnp.where(defers_upper, blocks // 4, 0))
    greeted = jnp.where(late & jnp.logical_not(leads), 1, shards - 1)
    awaited = (
        greeted
        + jnp.where(leads, blocks - deferred, 0)
        - jnp.where(serves_itself, 1, 0)
        + jnp.where(answers, shards, 0)
    )
    for step in range(1, shards):
        peer = lax.rem(src + step, shards)

        @pl.when(jnp.logical_not(late) | leads | (peer == head))
        def _():
            pl.semaphore_signal(barrier, inc=1, device_id=(blk, peer), device_id_type=MESH)

    for step in range(shards):
        @pl.when(jnp.logical_not(answers | (serves_itself & (slot == step))))
        def _():
            pl.semaphore_signal(
                barrier,
                inc=1,
                device_id=(src * shards + step, leader_of(src)),
                device_id_type=MESH,
            )

    def is_deferred(step):
        upper = lax.rem(lax.div(step, 4), 2) == 1
        return (step >= blocks // 2) & (defers_late | (defers_upper & upper))

    @pl.when(deferred > 0)
    def _():
        @pl.loop(blocks // 2, blocks)
        def _(step):
            @pl.when(is_deferred(step))
            def _():
                pl.semaphore_signal(
                    barrier, inc=1, device_id=(source_target(step), group), device_id_type=MESH
                )


    loads[0].wait()
    tap_high, tap_low = tap_matrix(taps[...], raw_count, out_rows + EDGE, out_rows)
    for load in loads[1:4]:
        load.wait()
    for load in loads[4:]:
        load.start()
    raw_high, raw_low = split(raw[...])
    decimated = dot_nt(tap_high, raw_high) + dot_nt(tap_low, raw_high) + dot_nt(tap_high, raw_low)
    decimated = decimated * alive[...].astype(F32)
    parts[src] = decimated

    lane = lax.broadcasted_iota(jnp.int32, (8, channels), 1)
    row = lax.broadcasted_iota(jnp.int32, (8, channels), 0)
    chosen = jnp.where(row == 0, index[0, 0], jnp.where(row == 1, index[0, 1], -1))
    chooser = (lane == chosen).astype(F32).astype(BF16)
    padded = jnp.concatenate(
        [
            decimated[:out_rows],
            jnp.zeros((LANES - out_rows - EDGE, channels), F32),
            decimated[out_rows:],
        ],
        axis=0,
    )
    first, rest = split(padded)
    second, third = split(padded - first.astype(F32))
    pieces[src] = dot_nt(chooser, first) + dot_nt(chooser, second) + dot_nt(chooser, third)

    def piece_copy(shard):
        return pltpu.make_async_remote_copy(
            src_ref=pieces.at[shard],
            dst_ref=pieces.at[shard],
            send_sem=piece_send,
            recv_sem=piece_recv.at[shard],
            device_id=(blk, head),
            device_id_type=MESH,
        )

    def part_copy(shard, sem, peer):
        return pltpu.make_async_remote_copy(
            src_ref=parts.at[shard],
            dst_ref=parts.at[shard],
            send_sem=part_send.at[sem],
            recv_sem=part_recv.at[shard],
            device_id=(blk, peer),
            device_id_type=MESH,
        )

    def own_part(step):
        other = lax.rem(chip + step, half)
        heard = jnp.where(other == lax.div(head, 2), 1 - lax.rem(head, 2), core)
        return part_copy(src, step, sibling if step == 0 else 2 * other + heard)

    def handed_part(step):
        of_core = step % 2
        shard = 2 * lax.rem(chip + 1 + step // 2, half) + of_core
        hands = jnp.logical_not(leads) & ((of_core == core) | (sibling == head))
        return shard, hands, part_copy(shard, half + step, sibling)

    def await_part(shard):
        pltpu.make_async_copy(parts.at[shard], parts.at[shard], part_recv.at[shard]).wait()

    def source_copy(step):
        target = source_target(step)
        return target, pltpu.make_async_remote_copy(
            src_ref=packed,
            dst_ref=arrived.at[slot],
            send_sem=source_send.at[step],
            recv_sem=source_recv.at[slot],
            device_id=(target, group),
            device_id_type=MESH,
        )

    def send_sources(start, stop, later):
        @pl.loop(start, stop)
        def _(step):
            target, copy = source_copy(step)
            turn = is_deferred(step) if later else jnp.logical_not(is_deferred(step))

            @pl.when(turn & ((target != blk) | (src != group)))
            def _():
                copy.start()

    def send_deferred():
        pl.semaphore_wait(ready, deferred)
        send_sources(blocks // 2, blocks, True)

    lane = lax.broadcasted_iota(jnp.int32, own_ref.shape, 1)
    channel = lax.broadcasted_iota(jnp.int32, own_ref.shape, 0)
    chosen = jnp.where(lane < shards, index[0, 0], index[0, 1])
    own = (lax.rem(lane, shards) == slot) & (lane < 2 * shards) & (channel == chosen)
    own_ref[...] = jnp.where(own & (src == group), 1.0, 0.0)

    pl.semaphore_wait(barrier, awaited)

    @pl.when(jnp.logical_not(leads))
    def _():
        piece_copy(src).start()

    @pl.when(answers)
    def _():
        for step in range(shards):
            pl.semaphore_signal(
                ready,
                inc=1,
                device_id=(src * shards + step, leader_of(src)),
                device_id_type=MESH,
            )

    def send_parts():
        for step in range(half):
            own_part(step).start()

    @pl.when(jnp.logical_not(late))
    def _():
        send_parts()

    @pl.when(leads)
    def _():
        for step in range(1, shards):
            shard = lax.rem(src + step, shards)
            pltpu.make_async_copy(pieces.at[shard], pieces.at[shard], piece_recv.at[shard]).wait()
        lane = lax.broadcasted_iota(jnp.int32, (8, LANES), 1)
        for pair in range(half):
            after = pieces[2 * pair + 2] if 2 * pair + 2 < shards else jnp.zeros((8, LANES), F32)
            joined = pltpu.roll(pieces[2 * pair + 1], LANES // 2, 1) + jnp.where(
                lane < LANES // 2, pieces[2 * pair], after
            )
            packed[pair : pair + 1, :] = joined[0:1]
            packed[half + pair : half + pair + 1, :] = joined[1:2]

        send_sources(0, blocks // 2, False)

        @pl.when(late)
        def _():
            for step in range(1, shards):
                peer = lax.rem(src + step, shards)
                pl.semaphore_signal(go, inc=1, device_id=(blk, peer), device_id_type=MESH)

            send_sources(blocks // 2, blocks, False)

        @pl.when(serves_itself)
        def _():
            arrived[slot] = packed[...]

    @pl.when(late)
    def _():
        @pl.when(jnp.logical_not(leads))
        def _():
            pl.semaphore_wait(go, 1)

        send_parts()

        @pl.when(defers_upper)
        def _():
            send_deferred()

    for step in range(shards - 2):
        shard, hands, copy = handed_part(step)

        @pl.when(hands)
        def _():
            await_part(shard)
            copy.start()

    for load in loads[4:]:
        load.wait()
    await_part(sibling)
    for step in range(shards - 2):
        shard, hands, copy = handed_part(step)

        @pl.when(jnp.logical_not(hands))
        def _():
            await_part(shard)

    rows = []
    for shard in range(shards):
        rows.append(parts[shard, : out_rows - EDGE])
        tail = parts[shard, out_rows - EDGE : out_rows]
        if shard + 1 < shards:
            tail = tail + parts[shard + 1, out_rows:]
        rows.append(tail)
    series = jnp.concatenate(rows, axis=0).T
    real_part, imag_part = whitened(series, high_table[...], low_table[...], band[...])
    receivers_ref[:, :BINS] = real_part
    receivers_ref[:, BINS:] = imag_part

    @pl.when(defers_late)
    def _():
        send_deferred()

    for step in range(shards):
        @pl.when(jnp.logical_not(serves_itself & (slot == step)))
        def _():
            pltpu.make_async_copy(arrived.at[step], arrived.at[step], source_recv.at[step]).wait()
    sources = jnp.concatenate(
        [
            jnp.concatenate([arrived[:, v * half + pair, :] for pair in range(half)], axis=1)
            for v in range(2)
        ],
        axis=0,
    )
    real_part, imag_part = whitened(sources, high_table[...], low_table[...], band[...])
    sources_ref[:, :BINS] = real_part
    sources_ref[:, BINS:] = imag_part

    for step in range(half):
        own_part(step).wait_send()
    for step in range(shards - 2):
        shard, hands, copy = handed_part(step)

        @pl.when(hands)
        def _():
            copy.wait_send()


    @pl.when(jnp.logical_not(leads))
    def _():
        piece_copy(src).wait_send()

    @pl.when(leads)
    def _():
        @pl.loop(0, blocks)
        def _(step):
            target, copy = source_copy(step)

            @pl.when((target != blk) | (src != group))
            def _():
                copy.wait_send()


def correlate_kernel(shards, group, receivers, sources, lags, own, out, cross, lagged, sem):
    channels = receivers.shape[0]
    count = sources.shape[0]

    def out_copy(row):
        local = lax.rem(row, shards) * 2 + lax.div(row, shards)
        return pltpu.make_async_copy(lagged.at[row], out.at[local], sem.at[row])

    def form(step):
        for k in range(group):
            row = step * group + k
            rows = pl.ds((step % 2 * group + k) * channels, channels)
            src_re, src_im = sources[row : row + 1, :BINS], sources[row : row + 1, BINS:]
            rec_re, rec_im = receivers[:, :BINS], receivers[:, BINS:]
            cross[rows, :BINS] = (src_re * rec_re + src_im * rec_im).astype(BF16)
            cross[rows, BINS:] = (src_re * rec_im - src_im * rec_re).astype(BF16)

    form(0)
    for step in range(count // group):
        if step + 1 < count // group:
            form(step + 1)
        size = group * channels
        product = dot(cross[pl.ds(step % 2 * size, size)], lags[...])
        for k in range(group):
            row = step * group + k
            same = own[:, row : row + 1] > 0.0
            kept = jnp.where(same, 0.0, product[k * channels : (k + 1) * channels])
            lagged[row] = kept.astype(BF16)
            out_copy(row).start()

    @pl.loop(0, count)
    def _(row):
        out_copy(row).wait()


def local(raw_records, fir_taps, alive_mask, source_index):
    shards = lax.axis_size("src")
    blocks = lax.axis_size("blk")
    channels, raw_count = raw_records.shape
    count = 2 * shards
    high_table, low_table = forward_tables()
    vmem = pl.BlockSpec(memory_space=pltpu.VMEM)
    hbm = pl.BlockSpec(memory_space=pltpu.HBM)
    dma = pltpu.SemaphoreType.DMA
    receivers, sources, own = pl.pallas_call(
        functools.partial(gather_kernel, shards, blocks),
        out_shape=(
            jax.ShapeDtypeStruct((channels, NFFT), F32),
            jax.ShapeDtypeStruct((count, NFFT), F32),
            jax.ShapeDtypeStruct((channels, LANES), F32),
        ),
        in_specs=[hbm] * 7,
        out_specs=(vmem, vmem, vmem),
        scratch_shapes=[
            pltpu.VMEM((channels, raw_count), F32),
            pltpu.VMEM((1, TAPS), F32),
            pltpu.VMEM((1, channels), jnp.int32),
            pltpu.SMEM((1, 2), jnp.int32),
            pltpu.VMEM((S, NFFT), BF16),
            pltpu.VMEM((S, NFFT), BF16),
            pltpu.VMEM((BINS, BINS), BF16),
            pltpu.VMEM((shards, S // shards + EDGE, channels), F32),
            pltpu.VMEM((shards, 8, LANES), F32),
            pltpu.VMEM((8, LANES), F32),
            pltpu.VMEM((shards, 8, LANES), F32),
            dma((7,)),
            dma,
            dma((shards,)),
            dma((shards // 2 + shards - 2,)),
            dma((shards,)),
            dma((blocks,)),
            dma((shards,)),
            pltpu.SemaphoreType.REGULAR,
            pltpu.SemaphoreType.REGULAR,
        ],
        compiler_params=pltpu.CompilerParams(
            collective_id=0, has_side_effects=True, vmem_limit_bytes=24 << 20
        ),
        name="gather_whiten",
    )(
        *(
            pltpu.with_memory_space_constraint(jnp.asarray(operand), pltpu.HBM)
            for operand in (
                raw_records,
                fir_taps.reshape(1, TAPS),
                alive_mask.reshape(1, channels),
                source_index,
                high_table,
                low_table,
                band_table(),
            )
        )
    )
    group = 2
    return pl.pallas_call(
        functools.partial(correlate_kernel, shards, group),
        out_shape=jax.ShapeDtypeStruct((count, channels, LAGS), BF16),
        in_specs=[vmem] * 4,
        out_specs=hbm,
        scratch_shapes=[
            pltpu.VMEM((2 * group * channels, NFFT), BF16),
            pltpu.VMEM((count, channels, LAGS), BF16),
            dma((count,)),
        ],
        compiler_params=pltpu.CompilerParams(vmem_limit_bytes=24 << 20),
        name="correlate",
    )(receivers, sources, lag_table(), own)


def solution(mesh):
    in_specs = (P("blk", "src"), P(), P("blk"), P("blk", None))
    out_specs = P("src", "blk", None)
    return jax.shard_map(local, mesh=mesh, in_specs=in_specs, out_specs=out_specs, check_vma=False)
```

```python
import functools
import math

import jax
import jax.numpy as jnp
import ml_dtypes
import numpy as np
from jax import lax
from jax.experimental import pallas as pl
from jax.experimental.pallas import tpu as pltpu
from jax.sharding import PartitionSpec as P

S = 512
NFFT = 1024
BINS = NFFT // 2
LAGS = 512
TAPS = 64
DEC = 20
HALF = 64
LANES = 128
EDGE = 8
MESH = pl.DeviceIdType.MESH
F32 = jnp.float32
BF16 = jnp.bfloat16


def split_np(table):
    high = table.astype(np.float32).astype(ml_dtypes.bfloat16)
    low = (table - high.astype(np.float64)).astype(ml_dtypes.bfloat16)
    return high, low


def forward_tables():
    phases = 2.0 * math.pi / NFFT * (np.outer(np.arange(S), np.arange(BINS)) % NFFT)
    return split_np(np.concatenate([np.cos(phases), -np.sin(phases)], axis=1))


def band_table():
    bins = np.arange(BINS)
    return (np.abs(bins[:, None] - bins[None, :]) <= HALF).astype(ml_dtypes.bfloat16)


def lag_table():
    bins = np.arange(BINS)
    shift = np.arange(LAGS) - LAGS // 2
    phases = 2.0 * math.pi / NFFT * (np.outer(bins, shift) % NFFT)
    weight = np.where(bins[:, None] == 0, 0.5, 1.0) / math.sqrt(BINS)
    table = np.concatenate([weight * np.cos(phases), -weight * np.sin(phases)], axis=0)
    return table.astype(np.float32).astype(ml_dtypes.bfloat16)


def split(value):
    high = value.astype(BF16)
    return high, (value - high.astype(F32)).astype(BF16)


def dot(a, b):
    return jnp.dot(a, b, preferred_element_type=F32)


def dot_nt(a, b):
    return lax.dot_general(a, b, (((1,), (1,)), ((), ())), preferred_element_type=F32)


def whitened(series, high_table, low_table, band):
    rows = series.shape[0]
    high, low = split(series)
    both = dot(jnp.concatenate([high, low], axis=0), high_table)
    spectrum = both[:rows] + both[rows:] + dot(high, low_table)
    real_part, imag_part = spectrum[:, :BINS], spectrum[:, BINS:]
    high, low = split(real_part * real_part + imag_part * imag_part)
    sums = dot(jnp.concatenate([high, low], axis=0), band)
    bins = lax.broadcasted_iota(jnp.int32, (1, BINS), 1)
    count = jnp.minimum(bins, HALF) + jnp.minimum(BINS - 1 - bins, HALF) + 1
    smooth = (sums[:rows] + sums[rows:]) / count.astype(F32)
    factor = lax.rsqrt(smooth + 1e-6)
    return real_part * factor, imag_part * factor


def tap_matrix(taps, raw_count, rows, edge_row):
    row = lax.broadcasted_iota(jnp.int32, (rows, LANES), 0)
    start = DEC * jnp.where(row < edge_row, row, row - rows)
    lane = lax.broadcasted_iota(jnp.int32, (rows, LANES), 1)
    padded = jnp.concatenate([taps, jnp.zeros((1, LANES - TAPS), F32)], axis=1)
    spread = jnp.broadcast_to(padded, (rows, LANES))
    turned = jnp.take_along_axis(spread, (lane - start) & (LANES - 1), axis=1)
    high, low = split(turned)
    high, low = high.astype(F32), low.astype(F32)
    highs, lows = [], []
    for first in range(0, raw_count, LANES):
        offset = lane + first - start
        inside = (offset >= 0) & (offset < TAPS)
        highs.append(jnp.where(inside, high, 0.0).astype(BF16))
        lows.append(jnp.where(inside, low, 0.0).astype(BF16))
    return jnp.concatenate(highs, axis=1), jnp.concatenate(lows, axis=1)


def leader_of(group):
    pair = lax.div(group, 2)
    return 2 * jnp.where(pair == 1, 2, jnp.where(pair == 3, 1, 0)) + lax.rem(group, 2)


def gather_kernel(
    shards,
    blocks,
    raw_hbm,
    taps_hbm,
    alive_hbm,
    index_hbm,
    high_hbm,
    low_hbm,
    band_hbm,
    receivers_ref,
    sources_ref,
    own_ref,
    raw,
    taps,
    alive,
    index,
    high_table,
    low_table,
    band,
    parts,
    pieces,
    packed,
    arrived,
    local_sem,
    piece_send,
    piece_recv,
    part_send,
    part_recv,
    source_send,
    source_recv,
    go,
    ready,
):
    blk = lax.axis_index("blk")
    src = lax.axis_index("src")
    channels, raw_count = raw.shape
    out_rows = S // shards
    half = shards // 2
    chip = lax.div(src, 2)
    core = lax.rem(src, 2)
    sibling = 2 * chip + 1 - core
    group = lax.div(blk, shards)
    slot = lax.rem(blk, shards)
    head = leader_of(group)
    leads = src == head
    serves_itself = leads & (src == group)
    late = lax.rem(lax.div(blk, 4), 8) >= 4

    def source_target(step):
        return lax.rem(lax.div(step, 4), 2) * (blocks // 2) + lax.div(step, 8) * 4 + lax.rem(step, 4)

    loads = [
        pltpu.make_async_copy(source, target, local_sem.at[k])
        for k, (source, target) in enumerate(
            [
                (taps_hbm, taps),
                (raw_hbm, raw),
                (alive_hbm, alive),
                (index_hbm, index),
                (high_hbm, high_table),
                (low_hbm, low_table),
                (band_hbm, band),
            ]
        )
    ]
    for load in loads[:4]:
        load.start()

    barrier = pltpu.get_barrier_semaphore()
    answers = late & (
        (lax.rem(src, half) < half // 2) | ((lax.div(src, 2) == 1) & (blk >= blocks // 2))
    )
    defers_late = leads & jnp.logical_not(late)
    defers_upper = leads & (lax.div(group, 2) == 1)
    deferred = jnp.where(defers_late, blocks // 2, jnp.where(defers_upper, blocks // 4, 0))
    greeted = jnp.where(late & jnp.logical_not(leads), 1, shards - 1)
    awaited = (
        greeted
        + jnp.where(leads, blocks - deferred, 0)
        - jnp.where(serves_itself, 1, 0)
        + jnp.where(answers, shards, 0)
    )
    for step in range(1, shards):
        peer = lax.rem(src + step, shards)

        @pl.when(jnp.logical_not(late) | leads | (peer == head))
        def _():
            pl.semaphore_signal(barrier, inc=1, device_id=(blk, peer), device_id_type=MESH)

    for step in range(shards):
        @pl.when(jnp.logical_not(answers | (serves_itself & (slot == step))))
        def _():
            pl.semaphore_signal(
                barrier,
                inc=1,
                device_id=(src * shards + step, leader_of(src)),
                device_id_type=MESH,
            )

    def is_deferred(step):
        upper = lax.rem(lax.div(step, 4), 2) == 1
        return (step >= blocks // 2) & (defers_late | (defers_upper & upper))

    @pl.when(deferred > 0)
    def _():
        @pl.loop(blocks // 2, blocks)
        def _(step):
            @pl.when(is_deferred(step))
            def _():
                pl.semaphore_signal(
                    barrier, inc=1, device_id=(source_target(step), group), device_id_type=MESH
                )


    loads[0].wait()
    tap_high, tap_low = tap_matrix(taps[...], raw_count, out_rows + EDGE, out_rows)
    for load in loads[1:4]:
        load.wait()
    for load in loads[4:]:
        load.start()
    raw_high, raw_low = split(raw[...])
    decimated = dot_nt(tap_high, raw_high) + dot_nt(tap_low, raw_high) + dot_nt(tap_high, raw_low)
    decimated = decimated * alive[...].astype(F32)
    parts[src] = decimated

    lane = lax.broadcasted_iota(jnp.int32, (8, channels), 1)
    row = lax.broadcasted_iota(jnp.int32, (8, channels), 0)
    chosen = jnp.where(row == 0, index[0, 0], jnp.where(row == 1, index[0, 1], -1))
    chooser = (lane == chosen).astype(F32).astype(BF16)
    padded = jnp.concatenate(
        [
            decimated[:out_rows],
            jnp.zeros((LANES - out_rows - EDGE, channels), F32),
            decimated[out_rows:],
        ],
        axis=0,
    )
    first, rest = split(padded)
    second, third = split(padded - first.astype(F32))
    pieces[src] = dot_nt(chooser, first) + dot_nt(chooser, second) + dot_nt(chooser, third)

    def piece_copy(shard):
        return pltpu.make_async_remote_copy(
            src_ref=pieces.at[shard],
            dst_ref=pieces.at[shard],
            send_sem=piece_send,
            recv_sem=piece_recv.at[shard],
            device_id=(blk, head),
            device_id_type=MESH,
        )

    def part_copy(shard, sem, peer):
        return pltpu.make_async_remote_copy(
            src_ref=parts.at[shard],
            dst_ref=parts.at[shard],
            send_sem=part_send.at[sem],
            recv_sem=part_recv.at[shard],
            device_id=(blk, peer),
            device_id_type=MESH,
        )

    def own_part(step):
        other = lax.rem(chip + step, half)
        heard = jnp.where(other == lax.div(head, 2), 1 - lax.rem(head, 2), core)
        return part_copy(src, step, sibling if step == 0 else 2 * other + heard)

    def handed_part(step):
        of_core = step % 2
        shard = 2 * lax.rem(chip + 1 + step // 2, half) + of_core
        hands = jnp.logical_not(leads) & ((of_core == core) | (sibling == head))
        return shard, hands, part_copy(shard, half + step, sibling)

    def await_part(shard):
        pltpu.make_async_copy(parts.at[shard], parts.at[shard], part_recv.at[shard]).wait()

    def source_copy(step):
        target = source_target(step)
        return target, pltpu.make_async_remote_copy(
            src_ref=packed,
            dst_ref=arrived.at[slot],
            send_sem=source_send.at[step],
            recv_sem=source_recv.at[slot],
            device_id=(target, group),
            device_id_type=MESH,
        )

    def send_sources(start, stop, later):
        @pl.loop(start, stop)
        def _(step):
            target, copy = source_copy(step)
            turn = is_deferred(step) if later else jnp.logical_not(is_deferred(step))

            @pl.when(turn & ((target != blk) | (src != group)))
            def _():
                copy.start()

    def send_deferred():
        pl.semaphore_wait(ready, deferred)
        send_sources(blocks // 2, blocks, True)

    row = lax.broadcasted_iota(jnp.int32, own_ref.shape, 0)
    chosen = jnp.where(row < shards, index[0, 0], index[0, 1])
    own_ref[...] = jnp.where((lax.rem(row, shards) == slot) & (src == group), chosen, -1)

    pl.semaphore_wait(barrier, awaited)

    @pl.when(jnp.logical_not(leads))
    def _():
        piece_copy(src).start()

    @pl.when(answers)
    def _():
        for step in range(shards):
            pl.semaphore_signal(
                ready,
                inc=1,
                device_id=(src * shards + step, leader_of(src)),
                device_id_type=MESH,
            )

    def send_parts():
        for step in range(half):
            own_part(step).start()

    @pl.when(jnp.logical_not(late))
    def _():
        send_parts()

    @pl.when(leads)
    def _():
        for step in range(1, shards):
            shard = lax.rem(src + step, shards)
            pltpu.make_async_copy(pieces.at[shard], pieces.at[shard], piece_recv.at[shard]).wait()
        lane = lax.broadcasted_iota(jnp.int32, (8, LANES), 1)
        for pair in range(half):
            after = pieces[2 * pair + 2] if 2 * pair + 2 < shards else jnp.zeros((8, LANES), F32)
            joined = pltpu.roll(pieces[2 * pair + 1], LANES // 2, 1) + jnp.where(
                lane < LANES // 2, pieces[2 * pair], after
            )
            packed[pair : pair + 1, :] = joined[0:1]
            packed[half + pair : half + pair + 1, :] = joined[1:2]

        send_sources(0, blocks // 2, False)

        @pl.when(late)
        def _():
            for step in range(1, shards):
                peer = lax.rem(src + step, shards)
                pl.semaphore_signal(go, inc=1, device_id=(blk, peer), device_id_type=MESH)

            send_sources(blocks // 2, blocks, False)

        @pl.when(serves_itself)
        def _():
            arrived[slot] = packed[...]

    @pl.when(late)
    def _():
        @pl.when(jnp.logical_not(leads))
        def _():
            pl.semaphore_wait(go, 1)

        send_parts()

        @pl.when(defers_upper)
        def _():
            send_deferred()

    for step in range(shards - 2):
        shard, hands, copy = handed_part(step)

        @pl.when(hands)
        def _():
            await_part(shard)
            copy.start()

    for load in loads[4:]:
        load.wait()
    await_part(sibling)
    for step in range(shards - 2):
        shard, hands, copy = handed_part(step)

        @pl.when(jnp.logical_not(hands))
        def _():
            await_part(shard)

    rows = []
    for shard in range(shards):
        rows.append(parts[shard, : out_rows - EDGE])
        tail = parts[shard, out_rows - EDGE : out_rows]
        if shard + 1 < shards:
            tail = tail + parts[shard + 1, out_rows:]
        rows.append(tail)
    series = jnp.concatenate(rows, axis=0).T
    real_part, imag_part = whitened(series, high_table[...], low_table[...], band[...])
    receivers_ref[:, :BINS] = real_part
    receivers_ref[:, BINS:] = imag_part

    @pl.when(defers_late)
    def _():
        send_deferred()

    for step in range(shards):
        @pl.when(jnp.logical_not(serves_itself & (slot == step)))
        def _():
            pltpu.make_async_copy(arrived.at[step], arrived.at[step], source_recv.at[step]).wait()
    sources = jnp.concatenate(
        [
            jnp.concatenate([arrived[:, v * half + pair, :] for pair in range(half)], axis=1)
            for v in range(2)
        ],
        axis=0,
    )
    real_part, imag_part = whitened(sources, high_table[...], low_table[...], band[...])
    sources_ref[:, :BINS] = real_part
    sources_ref[:, BINS:] = imag_part

    for step in range(half):
        own_part(step).wait_send()
    for step in range(shards - 2):
        shard, hands, copy = handed_part(step)

        @pl.when(hands)
        def _():
            copy.wait_send()


    @pl.when(jnp.logical_not(leads))
    def _():
        piece_copy(src).wait_send()

    @pl.when(leads)
    def _():
        @pl.loop(0, blocks)
        def _(step):
            target, copy = source_copy(step)

            @pl.when((target != blk) | (src != group))
            def _():
                copy.wait_send()


def correlate_kernel(shards, group, receivers, sources, lags, own, out, cross, lagged, sem):
    channels = receivers.shape[0]
    count = sources.shape[0]

    def out_copy(row):
        local = lax.rem(row, shards) * 2 + lax.div(row, shards)
        return pltpu.make_async_copy(lagged.at[row], out.at[local], sem.at[row])

    size = group * channels
    steps = count // group
    channel = lax.broadcasted_iota(jnp.int32, (channels, LAGS), 0)

    def form(step, place):
        for k in range(group):
            row = step * group + k
            rows = pl.ds((place * group + k) * channels, channels)
            src_re, src_im = sources[pl.ds(row, 1), :BINS], sources[pl.ds(row, 1), BINS:]
            rec_re, rec_im = receivers[:, :BINS], receivers[:, BINS:]
            cross[rows, :BINS] = (src_re * rec_re + src_im * rec_im).astype(BF16)
            cross[rows, BINS:] = (src_re * rec_im - src_im * rec_re).astype(BF16)

    form(0, 0)

    @pl.loop(0, steps // 2)
    def _(pair):
        for place in range(2):
            step = 2 * pair + place
            form(jnp.minimum(step + 1, steps - 1), 1 - place)
            product = dot(cross[pl.ds(place * size, size)], lags[...])
            for k in range(group):
                row = step * group + k
                part = product[k * channels : (k + 1) * channels]
                same = channel == own[pl.ds(row, 1), :]
                lagged[row] = jnp.where(same, 0.0, part).astype(BF16)
                out_copy(row).start()

    @pl.loop(0, count)
    def _(row):
        out_copy(row).wait()


def local(raw_records, fir_taps, alive_mask, source_index):
    shards = lax.axis_size("src")
    blocks = lax.axis_size("blk")
    channels, raw_count = raw_records.shape
    count = 2 * shards
    high_table, low_table = forward_tables()
    vmem = pl.BlockSpec(memory_space=pltpu.VMEM)
    hbm = pl.BlockSpec(memory_space=pltpu.HBM)
    dma = pltpu.SemaphoreType.DMA
    receivers, sources, own = pl.pallas_call(
        functools.partial(gather_kernel, shards, blocks),
        out_shape=(
            jax.ShapeDtypeStruct((channels, NFFT), F32),
            jax.ShapeDtypeStruct((count, NFFT), F32),
            jax.ShapeDtypeStruct((count, LAGS), jnp.int32),
        ),
        in_specs=[hbm] * 7,
        out_specs=(vmem, vmem, vmem),
        scratch_shapes=[
            pltpu.VMEM((channels, raw_count), F32),
            pltpu.VMEM((1, TAPS), F32),
            pltpu.VMEM((1, channels), jnp.int32),
            pltpu.SMEM((1, 2), jnp.int32),
            pltpu.VMEM((S, NFFT), BF16),
            pltpu.VMEM((S, NFFT), BF16),
            pltpu.VMEM((BINS, BINS), BF16),
            pltpu.VMEM((shards, S // shards + EDGE, channels), F32),
            pltpu.VMEM((shards, 8, LANES), F32),
            pltpu.VMEM((8, LANES), F32),
            pltpu.VMEM((shards, 8, LANES), F32),
            dma((7,)),
            dma,
            dma((shards,)),
            dma((shards // 2 + shards - 2,)),
            dma((shards,)),
            dma((blocks,)),
            dma((shards,)),
            pltpu.SemaphoreType.REGULAR,
            pltpu.SemaphoreType.REGULAR,
        ],
        compiler_params=pltpu.CompilerParams(
            collective_id=0, has_side_effects=True, vmem_limit_bytes=24 << 20
        ),
        name="gather_whiten",
    )(
        *(
            pltpu.with_memory_space_constraint(jnp.asarray(operand), pltpu.HBM)
            for operand in (
                raw_records,
                fir_taps.reshape(1, TAPS),
                alive_mask.reshape(1, channels),
                source_index,
                high_table,
                low_table,
                band_table(),
            )
        )
    )
    group = 2
    return pl.pallas_call(
        functools.partial(correlate_kernel, shards, group),
        out_shape=jax.ShapeDtypeStruct((count, channels, LAGS), BF16),
        in_specs=[vmem] * 4,
        out_specs=hbm,
        scratch_shapes=[
            pltpu.VMEM((2 * group * channels, NFFT), BF16),
            pltpu.VMEM((count, channels, LAGS), BF16),
            dma((count,)),
        ],
        compiler_params=pltpu.CompilerParams(vmem_limit_bytes=24 << 20),
        name="correlate",
    )(receivers, sources, lag_table(), own)


def solution(mesh):
    in_specs = (P("blk", "src"), P(), P("blk"), P("blk", None))
    out_specs = P("src", "blk", None)
    return jax.shard_map(local, mesh=mesh, in_specs=in_specs, out_specs=out_specs, check_vma=False)
```

```python
import functools
import math

import jax
import jax.numpy as jnp
import ml_dtypes
import numpy as np
from jax import lax
from jax.experimental import pallas as pl
from jax.experimental.pallas import tpu as pltpu
from jax.sharding import PartitionSpec as P

S = 512
NFFT = 1024
BINS = NFFT // 2
LAGS = 512
TAPS = 64
DEC = 20
HALF = 64
LANES = 128
EDGE = 8
MESH = pl.DeviceIdType.MESH
F32 = jnp.float32
BF16 = jnp.bfloat16


def split_np(table):
    high = table.astype(np.float32).astype(ml_dtypes.bfloat16)
    low = (table - high.astype(np.float64)).astype(ml_dtypes.bfloat16)
    return high, low


def forward_tables():
    phases = 2.0 * math.pi / NFFT * (np.outer(np.arange(S), np.arange(BINS)) % NFFT)
    return split_np(np.concatenate([np.cos(phases), -np.sin(phases)], axis=1))


def band_table():
    bins = np.arange(BINS)
    return (np.abs(bins[:, None] - bins[None, :]) <= HALF).astype(ml_dtypes.bfloat16)


def lag_table():
    bins = np.arange(BINS)
    shift = np.arange(LAGS) - LAGS // 2
    phases = 2.0 * math.pi / NFFT * (np.outer(bins, shift) % NFFT)
    weight = np.where(bins[:, None] == 0, 0.5, 1.0) / math.sqrt(BINS)
    table = np.concatenate([weight * np.cos(phases), -weight * np.sin(phases)], axis=0)
    return table.astype(np.float32).astype(ml_dtypes.bfloat16)


def split(value):
    high = value.astype(BF16)
    return high, (value - high.astype(F32)).astype(BF16)


def dot(a, b):
    return jnp.dot(a, b, preferred_element_type=F32)


def dot_nt(a, b):
    return lax.dot_general(a, b, (((1,), (1,)), ((), ())), preferred_element_type=F32)


def whitened(series, high_table, low_table, band):
    rows = series.shape[0]
    high, low = split(series)
    both = dot(jnp.concatenate([high, low], axis=0), high_table)
    spectrum = both[:rows] + both[rows:] + dot(high, low_table)
    real_part, imag_part = spectrum[:, :BINS], spectrum[:, BINS:]
    high, low = split(real_part * real_part + imag_part * imag_part)
    sums = dot(jnp.concatenate([high, low], axis=0), band)
    bins = lax.broadcasted_iota(jnp.int32, (1, BINS), 1)
    count = jnp.minimum(bins, HALF) + jnp.minimum(BINS - 1 - bins, HALF) + 1
    smooth = (sums[:rows] + sums[rows:]) / count.astype(F32)
    factor = lax.rsqrt(smooth + 1e-6)
    return real_part * factor, imag_part * factor


def tap_matrix(taps, raw_count, rows, edge_row):
    row = lax.broadcasted_iota(jnp.int32, (rows, LANES), 0)
    start = DEC * jnp.where(row < edge_row, row, row - rows)
    lane = lax.broadcasted_iota(jnp.int32, (rows, LANES), 1)
    padded = jnp.concatenate([taps, jnp.zeros((1, LANES - TAPS), F32)], axis=1)
    spread = jnp.broadcast_to(padded, (rows, LANES))
    turned = jnp.take_along_axis(spread, (lane - start) & (LANES - 1), axis=1)
    high, low = split(turned)
    high, low = high.astype(F32), low.astype(F32)
    highs, lows = [], []
    for first in range(0, raw_count, LANES):
        offset = lane + first - start
        inside = (offset >= 0) & (offset < TAPS)
        highs.append(jnp.where(inside, high, 0.0).astype(BF16))
        lows.append(jnp.where(inside, low, 0.0).astype(BF16))
    return jnp.concatenate(highs, axis=1), jnp.concatenate(lows, axis=1)


def leader_of(group):
    pair = lax.div(group, 2)
    return 2 * jnp.where(pair == 1, 2, jnp.where(pair == 3, 1, 0)) + lax.rem(group, 2)


def gather_kernel(
    shards,
    blocks,
    raw_hbm,
    taps_hbm,
    alive_hbm,
    index_hbm,
    high_hbm,
    low_hbm,
    band_hbm,
    receivers_ref,
    sources_ref,
    own_ref,
    raw,
    taps,
    alive,
    index,
    high_table,
    low_table,
    band,
    parts,
    pieces,
    packed,
    arrived,
    local_sem,
    piece_send,
    piece_recv,
    part_send,
    part_recv,
    source_send,
    source_recv,
    go,
    ready,
):
    blk = lax.axis_index("blk")
    src = lax.axis_index("src")
    channels, raw_count = raw.shape
    out_rows = S // shards
    half = shards // 2
    chip = lax.div(src, 2)
    core = lax.rem(src, 2)
    sibling = 2 * chip + 1 - core
    group = lax.div(blk, shards)
    slot = lax.rem(blk, shards)
    head = leader_of(group)
    leads = src == head
    serves_itself = leads & (src == group)
    late = lax.rem(lax.div(blk, 4), 8) >= 4

    def source_target(step):
        return lax.rem(lax.div(step, 4), 2) * (blocks // 2) + lax.div(step, 8) * 4 + lax.rem(step, 4)

    loads = [
        pltpu.make_async_copy(source, target, local_sem.at[k])
        for k, (source, target) in enumerate(
            [
                (taps_hbm, taps),
                (raw_hbm, raw),
                (alive_hbm, alive),
                (index_hbm, index),
                (high_hbm, high_table),
                (low_hbm, low_table),
                (band_hbm, band),
            ]
        )
    ]
    for load in loads[:4]:
        load.start()

    barrier = pltpu.get_barrier_semaphore()
    answers = late & (
        (lax.rem(src, half) < half // 2) | ((lax.div(src, 2) == 1) & (blk >= blocks // 2))
    )
    defers_late = leads & jnp.logical_not(late)
    defers_upper = leads & (lax.div(group, 2) == 1)
    deferred = jnp.where(defers_late, blocks // 2, jnp.where(defers_upper, blocks // 4, 0))
    greeted = jnp.where(late & jnp.logical_not(leads), 1, shards - 1)
    awaited = (
        greeted
        + jnp.where(leads, blocks - deferred, 0)
        - jnp.where(serves_itself, 1, 0)
        + jnp.where(answers, shards, 0)
    )
    for step in range(1, shards):
        peer = lax.rem(src + step, shards)

        @pl.when(jnp.logical_not(late) | leads | (peer == head))
        def _():
            pl.semaphore_signal(barrier, inc=1, device_id=(blk, peer), device_id_type=MESH)

    for step in range(shards):
        @pl.when(jnp.logical_not(answers | (serves_itself & (slot == step))))
        def _():
            pl.semaphore_signal(
                barrier,
                inc=1,
                device_id=(src * shards + step, leader_of(src)),
                device_id_type=MESH,
            )

    def is_deferred(step):
        upper = lax.rem(lax.div(step, 4), 2) == 1
        return (step >= blocks // 2) & (defers_late | (defers_upper & upper))

    @pl.when(deferred > 0)
    def _():
        @pl.loop(blocks // 2, blocks)
        def _(step):
            @pl.when(is_deferred(step))
            def _():
                pl.semaphore_signal(
                    barrier, inc=1, device_id=(source_target(step), group), device_id_type=MESH
                )


    loads[0].wait()
    tap_high, tap_low = tap_matrix(taps[...], raw_count, out_rows + EDGE, out_rows)
    for load in loads[1:4]:
        load.wait()
    for load in loads[4:]:
        load.start()
    raw_high, raw_low = split(raw[...])
    decimated = dot_nt(tap_high, raw_high) + dot_nt(tap_low, raw_high) + dot_nt(tap_high, raw_low)
    decimated = decimated * alive[...].astype(F32)
    parts[src] = decimated

    lane = lax.broadcasted_iota(jnp.int32, (8, channels), 1)
    row = lax.broadcasted_iota(jnp.int32, (8, channels), 0)
    chosen = jnp.where(row == 0, index[0, 0], jnp.where(row == 1, index[0, 1], -1))
    chooser = (lane == chosen).astype(F32).astype(BF16)
    padded = jnp.concatenate(
        [
            decimated[:out_rows],
            jnp.zeros((LANES - out_rows - EDGE, channels), F32),
            decimated[out_rows:],
        ],
        axis=0,
    )
    first, rest = split(padded)
    second, third = split(padded - first.astype(F32))
    pieces[src] = dot_nt(chooser, first) + dot_nt(chooser, second) + dot_nt(chooser, third)

    def piece_copy(shard):
        return pltpu.make_async_remote_copy(
            src_ref=pieces.at[shard],
            dst_ref=pieces.at[shard],
            send_sem=piece_send,
            recv_sem=piece_recv.at[shard],
            device_id=(blk, head),
            device_id_type=MESH,
        )

    def part_copy(shard, sem, peer):
        return pltpu.make_async_remote_copy(
            src_ref=parts.at[shard],
            dst_ref=parts.at[shard],
            send_sem=part_send.at[sem],
            recv_sem=part_recv.at[shard],
            device_id=(blk, peer),
            device_id_type=MESH,
        )

    def own_part(step):
        other = lax.rem(chip + step, half)
        heard = jnp.where(other == lax.div(head, 2), 1 - lax.rem(head, 2), core)
        return part_copy(src, step, sibling if step == 0 else 2 * other + heard)

    def handed_part(step):
        of_core = step % 2
        shard = 2 * lax.rem(chip + 1 + step // 2, half) + of_core
        hands = jnp.logical_not(leads) & ((of_core == core) | (sibling == head))
        return shard, hands, part_copy(shard, half + step, sibling)

    def await_part(shard):
        pltpu.make_async_copy(parts.at[shard], parts.at[shard], part_recv.at[shard]).wait()

    def source_copy(step):
        target = source_target(step)
        return target, pltpu.make_async_remote_copy(
            src_ref=packed,
            dst_ref=arrived.at[slot],
            send_sem=source_send.at[step],
            recv_sem=source_recv.at[slot],
            device_id=(target, group),
            device_id_type=MESH,
        )

    def send_sources(start, stop, later):
        @pl.loop(start, stop)
        def _(step):
            target, copy = source_copy(step)
            turn = is_deferred(step) if later else jnp.logical_not(is_deferred(step))

            @pl.when(turn & ((target != blk) | (src != group)))
            def _():
                copy.start()

    def send_deferred():
        pl.semaphore_wait(ready, deferred)
        send_sources(blocks // 2, blocks, True)

    lane = lax.broadcasted_iota(jnp.int32, own_ref.shape, 1)
    channel = lax.broadcasted_iota(jnp.int32, own_ref.shape, 0)
    chosen = jnp.where(lane < shards, index[0, 0], index[0, 1])
    own = (lax.rem(lane, shards) == slot) & (lane < 2 * shards) & (channel == chosen)
    own_ref[...] = jnp.where(own & (src == group), 1.0, 0.0)

    pl.semaphore_wait(barrier, awaited)

    @pl.when(jnp.logical_not(leads))
    def _():
        piece_copy(src).start()

    @pl.when(answers)
    def _():
        for step in range(shards):
            pl.semaphore_signal(
                ready,
                inc=1,
                device_id=(src * shards + step, leader_of(src)),
                device_id_type=MESH,
            )

    def send_parts():
        for step in range(half):
            own_part(step).start()

    @pl.when(jnp.logical_not(late))
    def _():
        send_parts()

    @pl.when(leads)
    def _():
        for step in range(1, shards):
            shard = lax.rem(src + step, shards)
            pltpu.make_async_copy(pieces.at[shard], pieces.at[shard], piece_recv.at[shard]).wait()
        lane = lax.broadcasted_iota(jnp.int32, (8, LANES), 1)
        for pair in range(half):
            after = pieces[2 * pair + 2] if 2 * pair + 2 < shards else jnp.zeros((8, LANES), F32)
            joined = pltpu.roll(pieces[2 * pair + 1], LANES // 2, 1) + jnp.where(
                lane < LANES // 2, pieces[2 * pair], after
            )
            packed[pair : pair + 1, :] = joined[0:1]
            packed[half + pair : half + pair + 1, :] = joined[1:2]

        send_sources(0, blocks // 2, False)

        @pl.when(late)
        def _():
            for step in range(1, shards):
                peer = lax.rem(src + step, shards)
                pl.semaphore_signal(go, inc=1, device_id=(blk, peer), device_id_type=MESH)

            send_sources(blocks // 2, blocks, False)

        @pl.when(serves_itself)
        def _():
            arrived[slot] = packed[...]

    @pl.when(late)
    def _():
        @pl.when(jnp.logical_not(leads))
        def _():
            pl.semaphore_wait(go, 1)

        send_parts()

        @pl.when(defers_upper)
        def _():
            send_deferred()

    for step in range(shards - 2):
        shard, hands, copy = handed_part(step)

        @pl.when(hands)
        def _():
            await_part(shard)
            copy.start()

    for load in loads[4:]:
        load.wait()
    await_part(sibling)
    for step in range(shards - 2):
        shard, hands, copy = handed_part(step)

        @pl.when(jnp.logical_not(hands))
        def _():
            await_part(shard)

    rows = []
    for shard in range(shards):
        rows.append(parts[shard, : out_rows - EDGE])
        tail = parts[shard, out_rows - EDGE : out_rows]
        if shard + 1 < shards:
            tail = tail + parts[shard + 1, out_rows:]
        rows.append(tail)
    series = jnp.concatenate(rows, axis=0).T
    real_part, imag_part = whitened(series, high_table[...], low_table[...], band[...])
    receivers_ref[:, :BINS] = real_part
    receivers_ref[:, BINS:] = imag_part

    @pl.when(defers_late)
    def _():
        send_deferred()

    for step in range(shards):
        @pl.when(jnp.logical_not(serves_itself & (slot == step)))
        def _():
            pltpu.make_async_copy(arrived.at[step], arrived.at[step], source_recv.at[step]).wait()
    sources = jnp.concatenate(
        [
            jnp.concatenate([arrived[:, v * half + pair, :] for pair in range(half)], axis=1)
            for v in range(2)
        ],
        axis=0,
    )
    real_part, imag_part = whitened(sources, high_table[...], low_table[...], band[...])
    sources_ref[:, :BINS] = real_part
    sources_ref[:, BINS:] = imag_part

    for step in range(half):
        own_part(step).wait_send()
    for step in range(shards - 2):
        shard, hands, copy = handed_part(step)

        @pl.when(hands)
        def _():
            copy.wait_send()


    @pl.when(jnp.logical_not(leads))
    def _():
        piece_copy(src).wait_send()

    @pl.when(leads)
    def _():
        @pl.loop(0, blocks)
        def _(step):
            target, copy = source_copy(step)

            @pl.when((target != blk) | (src != group))
            def _():
                copy.wait_send()


def correlate_kernel(shards, group, receivers, sources, lags, own, out, cross, lagged, sem):
    channels = receivers.shape[0]
    count = sources.shape[0]

    def out_copy(row):
        local = lax.rem(row, shards) * 2 + lax.div(row, shards)
        return pltpu.make_async_copy(lagged.at[row], out.at[local], sem.at[row])

    def form(step):
        for k in range(group):
            row = step * group + k
            rows = pl.ds((step % 2 * group + k) * channels, channels)
            src_re, src_im = sources[row : row + 1, :BINS], sources[row : row + 1, BINS:]
            rec_re, rec_im = receivers[:, :BINS], receivers[:, BINS:]
            cross[rows, :BINS] = (src_re * rec_re + src_im * rec_im).astype(BF16)
            cross[rows, BINS:] = (src_re * rec_im - src_im * rec_re).astype(BF16)

    form(0)
    for step in range(count // group):
        if step + 1 < count // group:
            form(step + 1)
        size = group * channels
        product = dot(cross[pl.ds(step % 2 * size, size)], lags[...])
        for k in range(group):
            row = step * group + k
            same = own[:, row : row + 1] > 0.0
            kept = jnp.where(same, 0.0, product[k * channels : (k + 1) * channels])
            lagged[row] = kept.astype(BF16)
            out_copy(row).start()

    @pl.loop(0, count)
    def _(row):
        out_copy(row).wait()


def local(raw_records, fir_taps, alive_mask, source_index):
    shards = lax.axis_size("src")
    blocks = lax.axis_size("blk")
    channels, raw_count = raw_records.shape
    count = 2 * shards
    high_table, low_table = forward_tables()
    vmem = pl.BlockSpec(memory_space=pltpu.VMEM)
    hbm = pl.BlockSpec(memory_space=pltpu.HBM)
    dma = pltpu.SemaphoreType.DMA
    receivers, sources, own = pl.pallas_call(
        functools.partial(gather_kernel, shards, blocks),
        out_shape=(
            jax.ShapeDtypeStruct((channels, NFFT), F32),
            jax.ShapeDtypeStruct((count, NFFT), F32),
            jax.ShapeDtypeStruct((channels, LANES), F32),
        ),
        in_specs=[hbm] * 7,
        out_specs=(vmem, vmem, vmem),
        scratch_shapes=[
            pltpu.VMEM((channels, raw_count), F32),
            pltpu.VMEM((1, TAPS), F32),
            pltpu.VMEM((1, channels), jnp.int32),
            pltpu.SMEM((1, 2), jnp.int32),
            pltpu.VMEM((S, NFFT), BF16),
            pltpu.VMEM((S, NFFT), BF16),
            pltpu.VMEM((BINS, BINS), BF16),
            pltpu.VMEM((shards, S // shards + EDGE, channels), F32),
            pltpu.VMEM((shards, 8, LANES), F32),
            pltpu.VMEM((8, LANES), F32),
            pltpu.VMEM((shards, 8, LANES), F32),
            dma((7,)),
            dma,
            dma((shards,)),
            dma((shards // 2 + shards - 2,)),
            dma((shards,)),
            dma((blocks,)),
            dma((shards,)),
            pltpu.SemaphoreType.REGULAR,
            pltpu.SemaphoreType.REGULAR,
        ],
        compiler_params=pltpu.CompilerParams(
            collective_id=0, has_side_effects=True, vmem_limit_bytes=24 << 20
        ),
        name="gather_whiten",
    )(
        *(
            pltpu.with_memory_space_constraint(jnp.asarray(operand), pltpu.HBM)
            for operand in (
                raw_records,
                fir_taps.reshape(1, TAPS),
                alive_mask.reshape(1, channels),
                source_index,
                high_table,
                low_table,
                band_table(),
            )
        )
    )
    group = 1
    return pl.pallas_call(
        functools.partial(correlate_kernel, shards, group),
        out_shape=jax.ShapeDtypeStruct((count, channels, LAGS), BF16),
        in_specs=[vmem] * 4,
        out_specs=hbm,
        scratch_shapes=[
            pltpu.VMEM((2 * group * channels, NFFT), BF16),
            pltpu.VMEM((count, channels, LAGS), BF16),
            dma((count,)),
        ],
        compiler_params=pltpu.CompilerParams(vmem_limit_bytes=24 << 20),
        name="correlate",
    )(receivers, sources, lag_table(), own)


def solution(mesh):
    in_specs = (P("blk", "src"), P(), P("blk"), P("blk", None))
    out_specs = P("src", "blk", None)
    return jax.shard_map(local, mesh=mesh, in_specs=in_specs, out_specs=out_specs, check_vma=False)
```
